32 devices in a mesh: dp: 16 (over z, y, x), tensor: 2 (over core).
Axes of the slice: x: 2, y: 2, z: 4, core: 2. Of those that a mesh axis runs over, the one named last changes fastest.
Arguments:
- activations: bfloat16 [8192, 8192], P('dp', 'tensor'), may hold values from -6 to 6
- out_grads: bfloat16 [8192, 16384], P('dp', 'tensor'), may hold values from -0.0625 to 0.0625
- sketch: float32 [8192, 512], P('dp'), may hold values from -6 to 6
- first_moment: float32 [512, 16384], P('dp', 'tensor'), may hold values from -6 to 6
- second_moment: float32 [512, 16384], P('dp', 'tensor'), may hold values from 0.05 to 2
Outputs:
- update: float32 [8192, 16384], P('dp', 'tensor')
- first_new: float32 [512, 16384], P('dp', 'tensor')
- second_new: float32 [512, 16384], P('dp', 'tensor')
The draws below stay inside these ranges and needn't reach their ends.
All inputs are finite; a program needn't handle non-finite values.
Results may differ from the reference program's by a relative error of at most 0.0041.
Values may be sent and summed in bfloat16 or wider, within the bound.
No kernel may reach another device: no remote copies, remote signals or barrier semaphores. Data moves between devices by JAX's collectives and lax.ppermute only.
A program may use at most 128 MiB of HBM per device.

```python
import math
import jax
import jax.numpy as jnp
from jax import lax

D = 8192
F = 16384
R = 512
TOKENS = 8192


def block_scale(own_key, dims, split, smallest, high):
    factor_of = 1.0
    for position, shards_of in split:
        steps = jax.random.uniform(jax.random.fold_in(jax.random.fold_in(own_key, 6), position), (shards_of,), jnp.float32, smallest / len(split), high / len(split))
        factor_of = factor_of * jnp.repeat(jnp.exp(steps), dims[position] // shards_of).reshape((-1,) + (1,) * (len(dims) - 1 - position))
    return factor_of


def centred(stream_key, shape, deviation, reach, shards=(), held_as=jnp.bfloat16):
    array = deviation * jax.random.normal(stream_key, shape, jnp.float32)
    if shards:
        array = array * block_scale(stream_key, shape, shards, -0.22, 0.18)
    return jnp.clip(array, -reach, reach).astype(held_as)


def setup_inputs(seed: int = 0) -> dict:
    key_list = jax.random.split(jax.random.key(seed), 6)
    return {
        "activations": centred(key_list[0], (TOKENS, D), 1.0, 6.0, ((0, 16), (1, 2))),
        "out_grads": centred(key_list[1], (TOKENS, F), TOKENS ** -0.5, 0.0625, ((0, 16), (1, 2))),
        "sketch": centred(key_list[2], (D, R), 1.0, 6.0, ((0, 16),), jnp.float32),
        "first_moment": centred(key_list[3], (R, F), 1.0, 6.0, ((0, 16), (1, 2)), jnp.float32),
        "second_moment": jnp.clip(jnp.exp(math.log(2.0) - 3.6888794 * jax.random.uniform(key_list[4], (R, F), jnp.float32) ** block_scale(key_list[4], (R, F), ((0, 16), (1, 2)), -0.2, 0.2)), 0.05, 2.0),
    }


BETA_ONE = 0.9
BETA_TWO = 0.999
CORRECT_ONE = 0.9999999993
CORRECT_TWO = 0.18135117
EPSILON = 1e-08

def reference(activations, out_grads, sketch, first_moment, second_moment):
    sketch_gram = jnp.dot(sketch.T.astype(jnp.float32), sketch.astype(jnp.float32), precision=lax.Precision.HIGHEST, preferred_element_type=jnp.float32)
    cholesky_factor = jnp.linalg.cholesky(sketch_gram)
    orthonormal = jax.scipy.linalg.solve_triangular(cholesky_factor, sketch.T, lower=True).T
    basis_low = orthonormal.astype(jnp.bfloat16)
    projected = jnp.dot(activations.astype(jnp.float32), basis_low.astype(jnp.float32), preferred_element_type=jnp.float32).astype(jnp.bfloat16)
    grad_low = jnp.dot(projected.T.astype(jnp.float32), out_grads.astype(jnp.float32), preferred_element_type=jnp.float32)
    first_new = BETA_ONE * first_moment + (1.0 - BETA_ONE) * grad_low
    second_new = BETA_TWO * second_moment + (1.0 - BETA_TWO) * grad_low * grad_low
    direction = (first_new / CORRECT_ONE / (jnp.sqrt(second_new / CORRECT_TWO) + EPSILON)).astype(jnp.bfloat16)
    update = math.sqrt(D / R) * jnp.dot(basis_low.astype(jnp.float32), direction.astype(jnp.float32), preferred_element_type=jnp.float32)
    return (update, first_new, second_new)
```

```python
import functools
import itertools
import math

import jax
import jax.numpy as jnp
from jax import lax
from jax.experimental import pallas as pl
from jax.experimental.pallas import tpu as pltpu
from jax.sharding import PartitionSpec as P

BETA_ONE = 0.9
BETA_TWO = 0.999
CORRECT_ONE = 0.9999999993
CORRECT_TWO = 0.18135117
EPSILON = 1e-08

HIGHEST = lax.Precision.HIGHEST
F32 = jnp.float32
BF16 = jnp.bfloat16
BLOCK = 128
PIVOTS = 8
VMEM_LIMIT = 40 << 20

GROUPS = ((2, (2, 1, 0)), (2, (1, 2, 0)), (2, (2, 1, 0)), (2, (1, 2, 0)))


def mesh_dims(devices):
    if devices == 16:
        return (4, 2, 2)
    if devices == 64:
        return (4, 4, 4)
    return (devices, 1, 1)


def shift_pairs(dims, shift):
    pairs = []
    for place in itertools.product(*(range(size) for size in dims)):
        target = [(at + by) % size for at, by, size in zip(place, shift, dims)]
        pairs.append((flat(place, dims), flat(target, dims)))
    return pairs


def flat(place, dims):
    index = 0
    for at, size in zip(place, dims):
        index = index * size + at
    return index


def send(value, dims, shift):
    return lax.ppermute(value, "dp", shift_pairs(dims, shift))


def unit(axis, by):
    return tuple(by if i == axis else 0 for i in range(3))


def dot_nn(a, b):
    return lax.dot_general(
        a, b, (((1,), (0,)), ((), ())), precision=HIGHEST, preferred_element_type=F32
    )


def dot_nt(a, b):
    return lax.dot_general(
        a, b, (((1,), (1,)), ((), ())), precision=HIGHEST, preferred_element_type=F32
    )


def inverse_factor(block):
    size = block.shape[0]
    tiles = size // 8
    lane = lax.broadcasted_iota(jnp.int32, (8, size), 1)
    sub = lax.broadcasted_iota(jnp.int32, (8, size), 0)
    spread = lambda value: jnp.broadcast_to(value, (8, size))
    work = [block[8 * i : 8 * i + 8, :] for i in range(tiles)]
    scale = [jnp.zeros((8, size), F32) for _ in range(tiles)]
    for base in range(0, size, PIVOTS):
        first = base // 8
        cols = {
            (i, k): spread(work[i][:, base + k : base + k + 1])
            for i in range(first, tiles)
            for k in range(PIVOTS)
        }
        for k in range(PIVOTS):
            j = base + k
            r, q = j % 8, j // 8
            pivot = spread(cols[q, k][r : r + 1, :])
            recip = 1.0 / pivot
            row = jnp.where(lane == j, 1.0, spread(work[q][r : r + 1, :]))
            later = {m: spread(cols[q, m][r : r + 1, :]) for m in range(k + 1, PIVOTS)}
            scale[q] = jnp.where(sub == r, pivot, scale[q])
            for i in range(q, tiles):
                ratio = cols[i, k] * recip
                cleared = lane == j
                if i == q:
                    ratio = jnp.where(sub > r, ratio, 0.0)
                    cleared = cleared & (sub > r)
                for m in range(k + 1, PIVOTS):
                    cols[i, m] = cols[i, m] - ratio * later[m]
                work[i] = jnp.where(cleared, 0.0, work[i]) - ratio * row
    out = []
    for i in range(tiles):
        at = sub + 8 * i
        lower = jnp.where(lane == at, 1.0, jnp.where(lane < at, work[i], 0.0))
        out.append(lower * lax.rsqrt(scale[i]))
    return jnp.concatenate(out, axis=0)


def lower_blocks(size):
    return [(i, j) for i in range(size // BLOCK) for j in range(i + 1)]


def factor_kernel(blocks, packed_ref, out_ref, work_ref):
    size = out_ref.shape[0]
    work_ref[...] = jnp.zeros_like(work_ref)
    for at, (i, j) in enumerate(blocks):
        work_ref[i * BLOCK : (i + 1) * BLOCK, j * BLOCK : (j + 1) * BLOCK] = packed_ref[
            at * BLOCK : (at + 1) * BLOCK, :
        ]
    out_ref[...] = jnp.where(
        lax.broadcasted_iota(jnp.int32, (size, size), 0)
        == lax.broadcasted_iota(jnp.int32, (size, size), 1),
        1.0,
        0.0,
    )

    def step(at, carry):
        base = pl.multiple_of(at * BLOCK, BLOCK)
        inverse = inverse_factor(work_ref[pl.ds(base, BLOCK), pl.ds(base, BLOCK)])
        rows = dot_nn(inverse, out_ref[pl.ds(base, BLOCK), :])
        out_ref[pl.ds(base, BLOCK), :] = rows

        @pl.when(at < size // BLOCK - 1)
        def _():
            panel = dot_nt(work_ref[:, pl.ds(base, BLOCK)], inverse)
            below = lax.broadcasted_iota(jnp.int32, (size, BLOCK), 0) >= base + BLOCK
            panel = jnp.where(below, panel, 0.0)
            work_ref[...] -= dot_nt(panel, panel)
            out_ref[...] -= dot_nn(panel, rows)

        return carry

    lax.fori_loop(0, size // BLOCK, step, 0)


def inverse_of_factor(packed, blocks, size):
    return pl.pallas_call(
        functools.partial(factor_kernel, blocks),
        out_shape=jax.ShapeDtypeStruct((size, size), F32),
        in_specs=[pl.BlockSpec(memory_space=pltpu.VMEM)],
        out_specs=pl.BlockSpec(memory_space=pltpu.VMEM),
        scratch_shapes=[pltpu.VMEM((size, size), F32)],
        compiler_params=pltpu.CompilerParams(vmem_limit_bytes=VMEM_LIMIT),
        name="inverse_factor",
    )(packed)


def summed_gram(sketch, dims, own, core):
    size = sketch.shape[1]
    blocks = lower_blocks(size)
    half = len(blocks) // 2
    gram = jnp.dot(sketch.T, sketch, precision=HIGHEST, preferred_element_type=F32)
    tiles = [
        gram[i * BLOCK : (i + 1) * BLOCK, j * BLOCK : (j + 1) * BLOCK] for i, j in blocks
    ]
    mine = jnp.where(
        core == 0, jnp.concatenate(tiles[:half]), jnp.concatenate(tiles[half:])
    )
    plane = dims[1] * dims[2]
    share = mine.shape[0] // plane
    at_of = lambda a, b: ((own[1] + a) % dims[1] * dims[2] + (own[2] + b) % dims[2]) * share
    shifts = list(itertools.product(range(dims[1]), range(dims[2])))
    part = lambda a, b: lax.dynamic_slice_in_dim(mine, at_of(a, b), share, 0)
    total = part(0, 0)
    arrived = [send(part(a, b), dims, (0, a, b)) for a, b in shifts[1:]]
    for piece in arrived:
        total = total + piece
    arrived = [send(total, dims, (by, 0, 0)) for by in range(1, dims[0])]
    places = jnp.stack([total] + arrived)
    order = [(own[0] - z) % dims[0] for z in range(dims[0])]
    total = functools.reduce(
        jnp.add, [lax.dynamic_index_in_dim(places, at, 0, keepdims=False) for at in order]
    )
    whole = lax.dynamic_update_slice_in_dim(
        jnp.zeros_like(mine), total, at_of(0, 0), 0
    )
    arrived = [send(total, dims, (0, -a, -b)) for a, b in shifts[1:]]
    for (a, b), piece in zip(shifts[1:], arrived):
        whole = lax.dynamic_update_slice_in_dim(whole, piece, at_of(a, b), 0)
    other = lax.ppermute(whole, "tensor", [(0, 1), (1, 0)])
    return (
        jnp.where(core == 0, jnp.concatenate([whole, other]), jnp.concatenate([other, whole])),
        blocks,
    )


def update_kernel(scale, count, *refs):
    weight_ref, pieces, out_ref = refs[0], refs[1 : 1 + count], refs[-1]
    rows = pieces[0].shape[0]
    total = None
    for at, piece in enumerate(pieces):
        term = jnp.dot(
            weight_ref[:, at * rows : (at + 1) * rows],
            piece[...],
            preferred_element_type=F32,
        )
        total = term if total is None else total + term
    out_ref[...] = scale * total


def update_columns(weight, pieces, previous, start, width, scale):
    tall, rank = weight.shape
    rows, cols = pieces[0].shape
    wide = min(1024, cols)
    first = start // wide
    in_specs = [pl.BlockSpec((tall, rank), lambda j: (0, 0))]
    in_specs += [pl.BlockSpec((rows, wide), lambda j: (0, j)) for _ in pieces]
    operands = [weight, *pieces]
    aliases = {}
    if previous is not None:
        aliases = {len(operands): 0}
        in_specs.append(pl.BlockSpec(memory_space=pl.ANY))
        operands.append(previous)
    return pl.pallas_call(
        functools.partial(update_kernel, scale, len(pieces)),
        grid=(cols // wide,),
        out_shape=jax.ShapeDtypeStruct((tall, width), F32),
        in_specs=in_specs,
        out_specs=pl.BlockSpec((tall, wide), lambda j: (0, first + j)),
        input_output_aliases=aliases,
        compiler_params=pltpu.CompilerParams(vmem_limit_bytes=VMEM_LIMIT),
        name="update_columns",
    )(*operands)


def selection(dims, own, order, rank, core):
    piece = rank // math.prod(dims)
    index = jnp.zeros((), jnp.int32)
    strides = (dims[1] * dims[2], dims[2], 1)
    for axis in order:
        places = (own[axis] + jnp.arange(dims[axis], dtype=jnp.int32)) % dims[axis]
        index = index[..., None] + places * strides[axis]
    index = index[..., None] * piece + jnp.arange(piece, dtype=jnp.int32)
    index = index.reshape(rank)
    return index


def one_hot(index, rank):
    return (index[:, None] == jnp.arange(rank, dtype=jnp.int32)[None, :]).astype(BF16)


def local(dims, activations, out_grads, sketch, first_moment, second_moment):
    dp = lax.axis_index("dp")
    core = lax.axis_index("tensor")
    own = (dp // (dims[1] * dims[2]), dp // dims[2] % dims[1], dp % dims[2])
    rank = sketch.shape[1]
    width = out_grads.shape[1]
    depth = activations.shape[1] * 2

    features = lax.all_gather(activations, "tensor", axis=1, tiled=True)
    half = lax.dynamic_slice_in_dim(sketch, core * (rank // 2), rank // 2, 1).astype(BF16)
    sketch_half = lax.all_gather(half, "dp", axis=0, tiled=True)
    mixed_half = jnp.dot(features, sketch_half, preferred_element_type=F32)
    mixed_other = lax.ppermute(mixed_half, "tensor", [(0, 1), (1, 0)])
    mixed = jnp.where(
        core == 0,
        jnp.concatenate([mixed_half, mixed_other], axis=1),
        jnp.concatenate([mixed_other, mixed_half], axis=1),
    )

    packed, blocks = summed_gram(sketch, dims, own, core)
    inverse = inverse_of_factor(packed, blocks, rank)
    own_rows = dot_nt(sketch, inverse).astype(BF16)
    projected = dot_nt(inverse, mixed).astype(BF16)

    selections = {}
    for _, order in GROUPS:
        if order not in selections:
            pick = one_hot(selection(dims, own, order, rank, core), rank)
            selections[order] = (
                jnp.dot(pick, projected, preferred_element_type=F32).astype(BF16),
                lax.dot_general(
                    own_rows, pick, (((1,), (1,)), ((), ())), preferred_element_type=F32
                ).astype(BF16),
            )

    update_scale = math.sqrt(depth / rank)
    eighth = width // 8
    start = 0
    states = []
    for share, order in GROUPS:
        cols = share * eighth
        grads = out_grads[:, start : start + cols]
        columns = selections[order][0]
        size = rank // dims[order[0]]
        term = lambda by: jnp.dot(
            columns[by * size : (by + 1) * size], grads, preferred_element_type=F32
        )
        axis = order[0]
        arrived = [
            send(term(by).astype(BF16), dims, unit(axis, by)) for by in range(1, dims[axis])
        ]
        total = term(0)
        for piece in arrived:
            total = total + piece.astype(F32)
        for axis in order[1:]:
            size = size // dims[axis]
            arrived = [
                send(total[by * size : (by + 1) * size].astype(BF16), dims, unit(axis, by))
                for by in range(1, dims[axis])
            ]
            total = total[:size]
            for piece in arrived:
                total = total + piece.astype(F32)
        states.append((start, cols, order, total))
        start += cols

    first_parts, second_parts = [], []
    update = None
    for start, cols, order, grad_low in states:
        first = BETA_ONE * first_moment[:, start : start + cols] + (1.0 - BETA_ONE) * grad_low
        second = (
            BETA_TWO * second_moment[:, start : start + cols]
            + (1.0 - BETA_TWO) * grad_low * grad_low
        )
        direction = (
            first / CORRECT_ONE / (jnp.sqrt(second / CORRECT_TWO) + EPSILON)
        ).astype(BF16)
        first_parts.append(first)
        second_parts.append(second)
        for axis in order[:0:-1]:
            direction = jnp.concatenate(
                [direction]
                + [send(direction, dims, unit(axis, -by)) for by in range(1, dims[axis])]
            )
        axis = order[0]
        pieces = [direction] + [
            send(direction, dims, unit(axis, -by)) for by in range(1, dims[axis])
        ]
        update = update_columns(
            selections[order][1], pieces, update, start, width, update_scale
        )
    return (
        update,
        jnp.concatenate(first_parts, axis=1),
        jnp.concatenate(second_parts, axis=1),
    )


def solution(mesh):
    dims = mesh_dims(mesh.shape["dp"])
    return jax.shard_map(
        functools.partial(local, dims),
        mesh=mesh,
        in_specs=(
            P("dp", "tensor"),
            P("dp", "tensor"),
            P("dp", None),
            P("dp", "tensor"),
            P("dp", "tensor"),
        ),
        out_specs=(P("dp", "tensor"), P("dp", "tensor"), P("dp", "tensor")),
        check_vma=False,
    )
```

```python
import functools
import itertools
import math

import jax
import jax.numpy as jnp
from jax import lax
from jax.experimental import pallas as pl
from jax.experimental.pallas import tpu as pltpu
from jax.sharding import PartitionSpec as P

BETA_ONE = 0.9
BETA_TWO = 0.999
CORRECT_ONE = 0.9999999993
CORRECT_TWO = 0.18135117
EPSILON = 1e-08

HIGHEST = lax.Precision.HIGHEST
F32 = jnp.float32
BF16 = jnp.bfloat16
BLOCK = 128
PIVOTS = 8
VMEM_LIMIT = 40 << 20

GROUPS = ((2, (0, 1, 2, 3)), (2, (2, 3, 1, 0)), (2, (1, 2, 0, 3)), (2, (0, 1, 2, 3)))
STEPS = ((0, 0), (1, 0), (2, 0), (3, 0), (0, 1), (1, 1), (2, 1), (0, 2), (3, 1), (1, 2), (2, 2), (0, 3), (3, 2), (1, 3), (2, 3), (0, 4), (3, 3), (1, 4), (2, 4), (0, 5), (1, 5), (3, 4), (2, 5), (0, 6), (1, 6), (3, 5), (2, 6), (0, 7), (3, 6), (1, 7), (2, 7), (3, 7), (0, 8), (1, 8), (2, 8), (3, 8))


def flip_pairs(devices, bit):
    return [(at, at ^ (1 << bit)) for at in range(devices)]


def flip(value, devices, bit):
    return lax.ppermute(value, "dp", flip_pairs(devices, bit))


def mesh_dims(devices):
    if devices == 16:
        return (4, 2, 2)
    if devices == 64:
        return (4, 4, 4)
    return (devices, 1, 1)


def shift_pairs(dims, shift):
    pairs = []
    for place in itertools.product(*(range(size) for size in dims)):
        target = [(at + by) % size for at, by, size in zip(place, shift, dims)]
        pairs.append((flat(place, dims), flat(target, dims)))
    return pairs


def flat(place, dims):
    index = 0
    for at, size in zip(place, dims):
        index = index * size + at
    return index


def send(value, dims, shift):
    return lax.ppermute(value, "dp", shift_pairs(dims, shift))


def dot_nn(a, b):
    return lax.dot_general(
        a, b, (((1,), (0,)), ((), ())), precision=HIGHEST, preferred_element_type=F32
    )


def dot_nt(a, b):
    return lax.dot_general(
        a, b, (((1,), (1,)), ((), ())), precision=HIGHEST, preferred_element_type=F32
    )


def inverse_factor(block):
    size = block.shape[0]
    tiles = size // 8
    lane = lax.broadcasted_iota(jnp.int32, (8, size), 1)
    sub = lax.broadcasted_iota(jnp.int32, (8, size), 0)
    spread = lambda value: jnp.broadcast_to(value, (8, size))
    work = [block[8 * i : 8 * i + 8, :] for i in range(tiles)]
    scale = [jnp.zeros((8, size), F32) for _ in range(tiles)]
    for base in range(0, size, PIVOTS):
        first = base // 8
        cols = {
            (i, k): spread(work[i][:, base + k : base + k + 1])
            for i in range(first, tiles)
            for k in range(PIVOTS)
        }
        for k in range(PIVOTS):
            j = base + k
            r, q = j % 8, j // 8
            pivot = spread(cols[q, k][r : r + 1, :])
            recip = 1.0 / pivot
            row = jnp.where(lane == j, 1.0, spread(work[q][r : r + 1, :]))
            later = {m: spread(cols[q, m][r : r + 1, :]) for m in range(k + 1, PIVOTS)}
            scale[q] = jnp.where(sub == r, pivot, scale[q])
            for i in range(q, tiles):
                ratio = cols[i, k] * recip
                cleared = lane == j
                if i == q:
                    ratio = jnp.where(sub > r, ratio, 0.0)
                    cleared = cleared & (sub > r)
                for m in range(k + 1, PIVOTS):
                    cols[i, m] = cols[i, m] - ratio * later[m]
                work[i] = jnp.where(cleared, 0.0, work[i]) - ratio * row
    out = []
    for i in range(tiles):
        at = sub + 8 * i
        lower = jnp.where(lane == at, 1.0, jnp.where(lane < at, work[i], 0.0))
        out.append(lower * lax.rsqrt(scale[i]))
    return jnp.concatenate(out, axis=0)


def lower_blocks(size):
    return [(i, j) for i in range(size // BLOCK) for j in range(i + 1)]


def factor_kernel(blocks, packed_ref, out_ref, work_ref):
    size = out_ref.shape[0]
    work_ref[...] = jnp.zeros_like(work_ref)
    for at, (i, j) in enumerate(blocks):
        work_ref[i * BLOCK : (i + 1) * BLOCK, j * BLOCK : (j + 1) * BLOCK] = packed_ref[
            at * BLOCK : (at + 1) * BLOCK, :
        ]
    out_ref[...] = jnp.where(
        lax.broadcasted_iota(jnp.int32, (size, size), 0)
        == lax.broadcasted_iota(jnp.int32, (size, size), 1),
        1.0,
        0.0,
    )

    def step(at, carry):
        base = pl.multiple_of(at * BLOCK, BLOCK)
        inverse = inverse_factor(work_ref[pl.ds(base, BLOCK), pl.ds(base, BLOCK)])
        rows = dot_nn(inverse, out_ref[pl.ds(base, BLOCK), :])
        out_ref[pl.ds(base, BLOCK), :] = rows

        @pl.when(at < size // BLOCK - 1)
        def _():
            panel = dot_nt(work_ref[:, pl.ds(base, BLOCK)], inverse)
            below = lax.broadcasted_iota(jnp.int32, (size, BLOCK), 0) >= base + BLOCK
            panel = jnp.where(below, panel, 0.0)
            work_ref[...] -= dot_nt(panel, panel)
            out_ref[...] -= dot_nn(panel, rows)

        return carry

    lax.fori_loop(0, size // BLOCK, step, 0)


def inverse_of_factor(packed, blocks, size):
    return pl.pallas_call(
        functools.partial(factor_kernel, blocks),
        out_shape=jax.ShapeDtypeStruct((size, size), F32),
        in_specs=[pl.BlockSpec(memory_space=pltpu.VMEM)],
        out_specs=pl.BlockSpec(memory_space=pltpu.VMEM),
        scratch_shapes=[pltpu.VMEM((size, size), F32)],
        compiler_params=pltpu.CompilerParams(vmem_limit_bytes=VMEM_LIMIT),
        name="inverse_factor",
    )(packed)


def summed_gram(sketch, dims, own, core):
    size = sketch.shape[1]
    blocks = lower_blocks(size)
    half = len(blocks) // 2
    gram = jnp.dot(sketch.T, sketch, precision=HIGHEST, preferred_element_type=F32)
    tiles = [
        gram[i * BLOCK : (i + 1) * BLOCK, j * BLOCK : (j + 1) * BLOCK] for i, j in blocks
    ]
    mine = jnp.where(
        core == 0, jnp.concatenate(tiles[:half]), jnp.concatenate(tiles[half:])
    )
    plane = dims[1] * dims[2]
    share = mine.shape[0] // plane
    at_of = lambda a, b: ((own[1] + a) % dims[1] * dims[2] + (own[2] + b) % dims[2]) * share
    shifts = list(itertools.product(range(dims[1]), range(dims[2])))
    part = lambda a, b: lax.dynamic_slice_in_dim(mine, at_of(a, b), share, 0)
    total = part(0, 0)
    arrived = [send(part(a, b), dims, (0, a, b)) for a, b in shifts[1:]]
    for piece in arrived:
        total = total + piece
    arrived = [send(total, dims, (by, 0, 0)) for by in range(1, dims[0])]
    places = jnp.stack([total] + arrived)
    order = [(own[0] - z) % dims[0] for z in range(dims[0])]
    total = functools.reduce(
        jnp.add, [lax.dynamic_index_in_dim(places, at, 0, keepdims=False) for at in order]
    )
    whole = lax.dynamic_update_slice_in_dim(
        jnp.zeros_like(mine), total, at_of(0, 0), 0
    )
    arrived = [send(total, dims, (0, -a, -b)) for a, b in shifts[1:]]
    for (a, b), piece in zip(shifts[1:], arrived):
        whole = lax.dynamic_update_slice_in_dim(whole, piece, at_of(a, b), 0)
    other = lax.ppermute(whole, "tensor", [(0, 1), (1, 0)])
    return (
        jnp.where(core == 0, jnp.concatenate([whole, other]), jnp.concatenate([other, whole])),
        blocks,
    )


def update_kernel(scale, count, *refs):
    weight_ref, pieces, out_ref = refs[0], refs[1 : 1 + count], refs[-1]
    rows = pieces[0].shape[0]
    total = None
    for at, piece in enumerate(pieces):
        term = jnp.dot(
            weight_ref[:, at * rows : (at + 1) * rows],
            piece[...],
            preferred_element_type=F32,
        )
        total = term if total is None else total + term
    out_ref[...] = scale * total


def update_columns(weight, pieces, previous, start, width, scale):
    tall, rank = weight.shape
    rows, cols = pieces[0].shape
    wide = min(1024, cols)
    first = start // wide
    in_specs = [pl.BlockSpec((tall, rank), lambda j: (0, 0))]
    in_specs += [pl.BlockSpec((rows, wide), lambda j: (0, j)) for _ in pieces]
    operands = [weight, *pieces]
    aliases = {}
    if previous is not None:
        aliases = {len(operands): 0}
        in_specs.append(pl.BlockSpec(memory_space=pl.ANY))
        operands.append(previous)
    return pl.pallas_call(
        functools.partial(update_kernel, scale, len(pieces)),
        grid=(cols // wide,),
        out_shape=jax.ShapeDtypeStruct((tall, width), F32),
        in_specs=in_specs,
        out_specs=pl.BlockSpec((tall, wide), lambda j: (0, first + j)),
        input_output_aliases=aliases,
        compiler_params=pltpu.CompilerParams(vmem_limit_bytes=VMEM_LIMIT),
        name="update_columns",
    )(*operands)


def selection(devices, dp, order, rank):
    index = jnp.zeros((), jnp.int32)
    for bit in order:
        index = index[..., None] | jnp.array([0, 1 << bit], jnp.int32)
    piece = rank // devices
    index = (index ^ dp)[..., None] * piece + jnp.arange(piece, dtype=jnp.int32)
    index = index.reshape(rank)
    return (index[:, None] == jnp.arange(rank, dtype=jnp.int32)[None, :]).astype(BF16)


def after(token, values):
    if token is None:
        return values
    return lax.optimization_barrier((*values, token))[:-1]


def local(dims, activations, out_grads, sketch, first_moment, second_moment):
    devices = math.prod(dims)
    bits = devices.bit_length() - 1
    dp = lax.axis_index("dp")
    core = lax.axis_index("tensor")
    own = (dp // (dims[1] * dims[2]), dp // dims[2] % dims[1], dp % dims[2])
    rank = sketch.shape[1]
    width = out_grads.shape[1]
    depth = activations.shape[1] * 2

    beside = lax.ppermute(activations, "tensor", [(0, 1), (1, 0)])
    half = lax.dynamic_slice_in_dim(sketch, core * (rank // 2), rank // 2, 1).astype(BF16)
    sketch_half = lax.all_gather(half, "dp", axis=0, tiled=True)
    mid = sketch_half.shape[0] // 2
    part = lambda at: lax.dynamic_slice_in_dim(sketch_half, at * mid, mid, 0)
    mixed_half = jnp.dot(activations, part(core), preferred_element_type=F32)
    mixed_half = mixed_half + jnp.dot(beside, part(1 - core), preferred_element_type=F32)
    mixed_other = lax.ppermute(mixed_half, "tensor", [(0, 1), (1, 0)])
    mixed = jnp.where(
        core == 0,
        jnp.concatenate([mixed_half, mixed_other], axis=1),
        jnp.concatenate([mixed_other, mixed_half], axis=1),
    )

    packed, blocks = summed_gram(sketch, dims, own, core)
    inverse = inverse_of_factor(packed, blocks, rank)
    own_rows = dot_nt(sketch, inverse).astype(BF16)
    projected = dot_nt(inverse, mixed).astype(BF16)

    orders = [order + tuple(range(4, bits)) for _, order in GROUPS]
    selections = {}
    for order in orders:
        if order not in selections:
            pick = selection(devices, dp, order, rank)
            selections[order] = (
                jnp.dot(pick, projected, preferred_element_type=F32).astype(BF16),
                lax.dot_general(
                    own_rows, pick, (((1,), (1,)), ((), ())), preferred_element_type=F32
                ).astype(BF16),
            )

    update_scale = math.sqrt(depth / rank)
    eighth = width // 8
    starts = [sum(share for share, _ in GROUPS[:g]) * eighth for g in range(len(GROUPS))]
    kept = [None] * len(GROUPS)
    arriving = [None] * len(GROUPS)
    first_parts = [None] * len(GROUPS)
    second_parts = [None] * len(GROUPS)
    token = None
    update = None
    last = 2 * bits
    steps = STEPS if STEPS and bits == 4 else [
        (g, s) for s in range(last + 1) for g in range(len(GROUPS))
    ]
    for g, step in steps:
        order = orders[g]
        cols = GROUPS[g][0] * eighth
        start = starts[g]
        columns = slice(start, start + cols)
        if step == 0:
            size = rank // 2
            left, grads = after(token, (selections[order][0], out_grads))
            outgoing = jnp.dot(
                left[size:], grads[:, columns], preferred_element_type=F32
            ).astype(BF16)
            kept[g] = jnp.dot(left[:size], grads[:, columns], preferred_element_type=F32)
            bit = order[0]
        elif step < bits:
            total, piece = after(token, (kept[g], arriving[g]))
            total = total + piece.astype(F32)
            size = total.shape[0] // 2
            outgoing = total[size:].astype(BF16)
            kept[g] = total[:size]
            bit = order[step]
        elif step == bits:
            total, piece = after(token, (kept[g], arriving[g]))
            grad_low = total + piece.astype(F32)
            first = BETA_ONE * first_moment[:, columns] + (1.0 - BETA_ONE) * grad_low
            second = (
                BETA_TWO * second_moment[:, columns]
                + (1.0 - BETA_TWO) * grad_low * grad_low
            )
            outgoing = (
                first / CORRECT_ONE / (jnp.sqrt(second / CORRECT_TWO) + EPSILON)
            ).astype(BF16)
            first_parts[g], second_parts[g] = first, second
            kept[g] = outgoing
            bit = order[bits - 1]
        elif step < last:
            mine, piece = after(token, (kept[g], arriving[g]))
            outgoing = kept[g] = jnp.concatenate([mine, piece])
            bit = order[last - 1 - step]
        else:
            pieces = after(token, (kept[g], arriving[g]))
            update = update_columns(
                selections[order][1], pieces, update, start, width, update_scale
            )
            continue
        arriving[g] = flip(outgoing, devices, bit)
        token = outgoing
    return (
        update,
        jnp.concatenate(first_parts, axis=1),
        jnp.concatenate(second_parts, axis=1),
    )


def solution(mesh):
    dims = mesh_dims(mesh.shape["dp"])
    return jax.shard_map(
        functools.partial(local, dims),
        mesh=mesh,
        in_specs=(
            P("dp", "tensor"),
            P("dp", "tensor"),
            P("dp", None),
            P("dp", "tensor"),
            P("dp", "tensor"),
        ),
        out_specs=(P("dp", "tensor"), P("dp", "tensor"), P("dp", "tensor")),
        check_vma=False,
    )
```

```python
import functools
import itertools
import math

import jax
import jax.numpy as jnp
from jax import lax
from jax.experimental import pallas as pl
from jax.experimental.pallas import tpu as pltpu
from jax.sharding import PartitionSpec as P

BETA_ONE = 0.9
BETA_TWO = 0.999
CORRECT_ONE = 0.9999999993
CORRECT_TWO = 0.18135117
EPSILON = 1e-08

HIGHEST = lax.Precision.HIGHEST
F32 = jnp.float32
BF16 = jnp.bfloat16
BLOCK = 128
PIVOTS = 8
VMEM_LIMIT = 40 << 20

GROUPS = ((2, (0, 1, 2, 3)), (2, (2, 3, 1, 0)), (2, (1, 2, 0, 3)), (2, (0, 1, 2, 3)))
STEPS = ((0, 0), (1, 0), (2, 0), (3, 0), (0, 1), (1, 1), (2, 1), (0, 2), (3, 1), (1, 2), (2, 2), (0, 3), (3, 2), (1, 3), (2, 3), (0, 4), (3, 3), (1, 4), (2, 4), (0, 5), (1, 5), (3, 4), (2, 5), (0, 6), (1, 6), (3, 5), (2, 6), (0, 7), (3, 6), (1, 7), (2, 7), (3, 7), (0, 8), (1, 8), (2, 8), (3, 8))


GATHER = ((0, 1, 2, 3), (1, 0, 2, 3), (2, 1, 0, 3), (2, 0, 1, 3))


def flip_pairs(devices, bit):
    return [(at, at ^ (1 << bit)) for at in range(devices)]


def flip(value, devices, bit):
    return lax.ppermute(value, "dp", flip_pairs(devices, bit))


def mesh_dims(devices):
    if devices == 16:
        return (4, 2, 2)
    if devices == 64:
        return (4, 4, 4)
    return (devices, 1, 1)


def shift_pairs(dims, shift):
    pairs = []
    for place in itertools.product(*(range(size) for size in dims)):
        target = [(at + by) % size for at, by, size in zip(place, shift, dims)]
        pairs.append((flat(place, dims), flat(target, dims)))
    return pairs


def flat(place, dims):
    index = 0
    for at, size in zip(place, dims):
        index = index * size + at
    return index


def send(value, dims, shift):
    return lax.ppermute(value, "dp", shift_pairs(dims, shift))


def dot_nn(a, b):
    return lax.dot_general(
        a, b, (((1,), (0,)), ((), ())), precision=HIGHEST, preferred_element_type=F32
    )


def dot_nt(a, b):
    return lax.dot_general(
        a, b, (((1,), (1,)), ((), ())), precision=HIGHEST, preferred_element_type=F32
    )


def inverse_factor(block):
    size = block.shape[0]
    tiles = size // 8
    lane = lax.broadcasted_iota(jnp.int32, (8, size), 1)
    sub = lax.broadcasted_iota(jnp.int32, (8, size), 0)
    spread = lambda value: jnp.broadcast_to(value, (8, size))
    work = [block[8 * i : 8 * i + 8, :] for i in range(tiles)]
    scale = [jnp.zeros((8, size), F32) for _ in range(tiles)]
    for base in range(0, size, PIVOTS):
        first = base // 8
        cols = {
            (i, k): spread(work[i][:, base + k : base + k + 1])
            for i in range(first, tiles)
            for k in range(PIVOTS)
        }
        for k in range(PIVOTS):
            j = base + k
            r, q = j % 8, j // 8
            pivot = spread(cols[q, k][r : r + 1, :])
            recip = 1.0 / pivot
            row = jnp.where(lane == j, 1.0, spread(work[q][r : r + 1, :]))
            later = {m: spread(cols[q, m][r : r + 1, :]) for m in range(k + 1, PIVOTS)}
            scale[q] = jnp.where(sub == r, pivot, scale[q])
            for i in range(q, tiles):
                ratio = cols[i, k] * recip
                cleared = lane == j
                if i == q:
                    ratio = jnp.where(sub > r, ratio, 0.0)
                    cleared = cleared & (sub > r)
                for m in range(k + 1, PIVOTS):
                    cols[i, m] = cols[i, m] - ratio * later[m]
                work[i] = jnp.where(cleared, 0.0, work[i]) - ratio * row
    out = []
    for i in range(tiles):
        at = sub + 8 * i
        lower = jnp.where(lane == at, 1.0, jnp.where(lane < at, work[i], 0.0))
        out.append(lower * lax.rsqrt(scale[i]))
    return jnp.concatenate(out, axis=0)


def lower_blocks(size):
    return [(i, j) for i in range(size // BLOCK) for j in range(i + 1)]


def factor_kernel(blocks, packed_ref, out_ref, work_ref):
    size = out_ref.shape[0]
    work_ref[...] = jnp.zeros_like(work_ref)
    for at, (i, j) in enumerate(blocks):
        work_ref[i * BLOCK : (i + 1) * BLOCK, j * BLOCK : (j + 1) * BLOCK] = packed_ref[
            at * BLOCK : (at + 1) * BLOCK, :
        ]
    out_ref[...] = jnp.where(
        lax.broadcasted_iota(jnp.int32, (size, size), 0)
        == lax.broadcasted_iota(jnp.int32, (size, size), 1),
        1.0,
        0.0,
    )

    def step(at, carry):
        base = pl.multiple_of(at * BLOCK, BLOCK)
        inverse = inverse_factor(work_ref[pl.ds(base, BLOCK), pl.ds(base, BLOCK)])
        rows = dot_nn(inverse, out_ref[pl.ds(base, BLOCK), :])
        out_ref[pl.ds(base, BLOCK), :] = rows

        @pl.when(at < size // BLOCK - 1)
        def _():
            panel = dot_nt(work_ref[:, pl.ds(base, BLOCK)], inverse)
            below = lax.broadcasted_iota(jnp.int32, (size, BLOCK), 0) >= base + BLOCK
            panel = jnp.where(below, panel, 0.0)
            work_ref[...] -= dot_nt(panel, panel)
            out_ref[...] -= dot_nn(panel, rows)

        return carry

    lax.fori_loop(0, size // BLOCK, step, 0)


def inverse_of_factor(packed, blocks, size):
    return pl.pallas_call(
        functools.partial(factor_kernel, blocks),
        out_shape=jax.ShapeDtypeStruct((size, size), F32),
        in_specs=[pl.BlockSpec(memory_space=pltpu.VMEM)],
        out_specs=pl.BlockSpec(memory_space=pltpu.VMEM),
        scratch_shapes=[pltpu.VMEM((size, size), F32)],
        compiler_params=pltpu.CompilerParams(vmem_limit_bytes=VMEM_LIMIT),
        name="inverse_factor",
    )(packed)


def gram_and_sketch(sketch, half, dims, own, core):
    devices = math.prod(dims)
    bits = devices.bit_length() - 1
    size = sketch.shape[1]
    blocks = lower_blocks(size)
    split = len(blocks) // 2
    gram = jnp.dot(sketch.T, sketch, precision=HIGHEST, preferred_element_type=F32)
    tiles = [
        gram[i * BLOCK : (i + 1) * BLOCK, j * BLOCK : (j + 1) * BLOCK] for i, j in blocks
    ]
    mine = jnp.where(
        core == 0, jnp.concatenate(tiles[:split]), jnp.concatenate(tiles[split:])
    )
    plane = dims[1] * dims[2]
    share = mine.shape[0] // plane
    at_of = lambda a, b: ((own[1] + a) % dims[1] * dims[2] + (own[2] + b) % dims[2]) * share
    shifts = list(itertools.product(range(dims[1]), range(dims[2])))
    part = lambda a, b: lax.dynamic_slice_in_dim(mine, at_of(a, b), share, 0)
    outgoing = [part(a, b) for a, b in shifts[1:]]
    total = part(0, 0)
    arrived = [send(piece, dims, (0, a, b)) for (a, b), piece in zip(shifts[1:], outgoing)]

    groups = gather_groups(half.shape[0], bits)
    tall = half.shape[0] // len(groups)
    (half,) = after(outgoing[-1], (half,))
    gathered = [half[None, g * tall : (g + 1) * tall] for g in range(len(groups))]
    moving = [flip(rows, devices, order[-1]) for rows, order in zip(gathered, groups)]

    def widen(stage, token):
        for g, order in enumerate(groups):
            rows, piece = after(token, (gathered[g], moving[g]))
            token = gathered[g] = jnp.concatenate([rows, piece])
            moving[g] = flip(token, devices, order[-1 - stage])
        return token

    arrived = after(half, arrived)
    for piece in arrived:
        total = total + piece
    arrived = [send(total, dims, (by, 0, 0)) for by in range(1, dims[0])]
    token = widen(1, total)
    arrived = after(token, arrived)
    places = jnp.stack([total, *arrived])
    order = [(own[0] - z) % dims[0] for z in range(dims[0])]
    total = functools.reduce(
        jnp.add, [lax.dynamic_index_in_dim(places, at, 0, keepdims=False) for at in order]
    )
    arrived = [send(total, dims, (0, -a, -b)) for a, b in shifts[1:]]
    token = widen(2, total)
    arrived = after(token, arrived)
    whole = lax.dynamic_update_slice_in_dim(
        jnp.zeros_like(mine), total, at_of(0, 0), 0
    )
    for (a, b), piece in zip(shifts[1:], arrived):
        whole = lax.dynamic_update_slice_in_dim(whole, piece, at_of(a, b), 0)
    other = lax.ppermute(whole, "tensor", [(0, 1), (1, 0)])
    token = whole
    for stage in range(3, bits):
        token = widen(stage, token)
    whole, other = after(token, (whole, other))
    packed = jnp.where(
        core == 0, jnp.concatenate([whole, other]), jnp.concatenate([other, whole])
    )
    return packed, blocks, groups, gathered, moving


def gather_groups(rows, bits):
    count = max(1, min(len(GATHER), rows // BLOCK))
    return [order + tuple(range(4, bits)) for order in GATHER[:count]]


def mix_kernel(groups, limit, table_ref, left_ref, right_ref, *refs):
    at = pl.program_id(0)
    out_ref = refs[-1]
    tall = refs[0].shape[1]
    total = None
    for side, source in enumerate((left_ref, right_ref)):
        for g in range(groups):
            near, far = refs[2 * (side * groups + g)], refs[2 * (side * groups + g) + 1]
            place = table_ref[side, g, at]
            rows = jnp.where(place < limit, near[0], far[0])
            term = jnp.dot(
                source[:, g * tall : (g + 1) * tall], rows, preferred_element_type=F32
            )
            total = term if total is None else total + term

    @pl.when(at == 0)
    def _():
        out_ref[...] = total

    @pl.when(at > 0)
    def _():
        out_ref[...] += total


def mix(left, right, near, far, groups, dp, core):
    limit, tall, cols = near[0].shape
    bits = limit.bit_length()
    count = len(groups)
    blocks = jnp.arange(limit, dtype=jnp.int32)
    table = []
    for side in (core, 1 - core):
        apart = (side * limit + blocks) ^ dp
        row = []
        for order in groups:
            place = jnp.zeros_like(apart)
            for bit in order:
                place = place * 2 + ((apart >> bit) & 1)
            row.append(place)
        table.append(jnp.stack(row))
    table = jnp.stack(table)
    block = left.shape[1] // limit
    in_specs = [pl.BlockSpec((left.shape[0], block), lambda i, t: (0, i))] * 2
    operands = [left, right]
    for side in range(2):
        for g in range(count):
            spec = pl.BlockSpec(
                (1, tall, cols),
                lambda i, t, side=side, g=g: (t[side, g, i] % limit, 0, 0),
            )
            in_specs += [spec, spec]
            operands += [near[g], far[g]]
    return pl.pallas_call(
        functools.partial(mix_kernel, count, limit),
        grid_spec=pltpu.PrefetchScalarGridSpec(
            num_scalar_prefetch=1,
            grid=(limit,),
            in_specs=in_specs,
            out_specs=pl.BlockSpec((left.shape[0], cols), lambda i, t: (0, 0)),
        ),
        out_shape=jax.ShapeDtypeStruct((left.shape[0], cols), F32),
        compiler_params=pltpu.CompilerParams(vmem_limit_bytes=VMEM_LIMIT),
        name="mix",
    )(table, *operands)


def update_kernel(scale, count, *refs):
    weight_ref, pieces, out_ref = refs[0], refs[1 : 1 + count], refs[-1]
    rows = pieces[0].shape[0]
    total = None
    for at, piece in enumerate(pieces):
        term = jnp.dot(
            weight_ref[:, at * rows : (at + 1) * rows],
            piece[...],
            preferred_element_type=F32,
        )
        total = term if total is None else total + term
    out_ref[...] = scale * total


def update_columns(weight, pieces, previous, start, width, scale):
    tall, rank = weight.shape
    rows, cols = pieces[0].shape
    wide = min(1024, cols)
    first = start // wide
    in_specs = [pl.BlockSpec((tall, rank), lambda j: (0, 0))]
    in_specs += [pl.BlockSpec((rows, wide), lambda j: (0, j)) for _ in pieces]
    operands = [weight, *pieces]
    aliases = {}
    if previous is not None:
        aliases = {len(operands): 0}
        in_specs.append(pl.BlockSpec(memory_space=pl.ANY))
        operands.append(previous)
    return pl.pallas_call(
        functools.partial(update_kernel, scale, len(pieces)),
        grid=(cols // wide,),
        out_shape=jax.ShapeDtypeStruct((tall, width), F32),
        in_specs=in_specs,
        out_specs=pl.BlockSpec((tall, wide), lambda j: (0, first + j)),
        input_output_aliases=aliases,
        compiler_params=pltpu.CompilerParams(vmem_limit_bytes=VMEM_LIMIT),
        name="update_columns",
    )(*operands)


def selection(devices, dp, order, rank):
    index = jnp.zeros((), jnp.int32)
    for bit in order:
        index = index[..., None] | jnp.array([0, 1 << bit], jnp.int32)
    piece = rank // devices
    index = (index ^ dp)[..., None] * piece + jnp.arange(piece, dtype=jnp.int32)
    index = index.reshape(rank)
    return (index[:, None] == jnp.arange(rank, dtype=jnp.int32)[None, :]).astype(BF16)


def after(token, values):
    if token is None:
        return values
    return lax.optimization_barrier((*values, token))[:-1]


def local(dims, activations, out_grads, sketch, first_moment, second_moment):
    devices = math.prod(dims)
    bits = devices.bit_length() - 1
    dp = lax.axis_index("dp")
    core = lax.axis_index("tensor")
    own = (dp // (dims[1] * dims[2]), dp // dims[2] % dims[1], dp % dims[2])
    rank = sketch.shape[1]
    width = out_grads.shape[1]
    depth = activations.shape[1] * 2

    beside = lax.ppermute(activations, "tensor", [(0, 1), (1, 0)])
    half = lax.dynamic_slice_in_dim(sketch, core * (rank // 2), rank // 2, 1).astype(BF16)
    packed, blocks, groups, near, far = gram_and_sketch(sketch, half, dims, own, core)
    inverse = inverse_of_factor(packed, blocks, rank)
    *far, activations = after(inverse, (*far, activations))
    mixed_half = mix(activations, beside, near, far, groups, dp, core)
    mixed_other = lax.ppermute(mixed_half, "tensor", [(0, 1), (1, 0)])
    mixed = jnp.where(
        core == 0,
        jnp.concatenate([mixed_half, mixed_other], axis=1),
        jnp.concatenate([mixed_other, mixed_half], axis=1),
    )

    orders = [order + tuple(range(4, bits)) for _, order in GROUPS]
    picks = {order: selection(devices, dp, order, rank) for order in orders}
    projected, weights = {}, {}
    update_scale = math.sqrt(depth / rank)
    eighth = width // 8
    starts = [sum(share for share, _ in GROUPS[:g]) * eighth for g in range(len(GROUPS))]
    kept = [None] * len(GROUPS)
    arriving = [None] * len(GROUPS)
    first_parts = [None] * len(GROUPS)
    second_parts = [None] * len(GROUPS)
    token = None
    update = None
    last = 2 * bits
    steps = STEPS if STEPS and bits == 4 else [
        (g, s) for s in range(last + 1) for g in range(len(GROUPS))
    ]
    for g, step in steps:
        order = orders[g]
        if step == 1 and not weights:
            rows, factor = after(token, (sketch, inverse))
            own_rows = dot_nt(rows, factor).astype(BF16)
            for each, pick in picks.items():
                weights[each] = lax.dot_general(
                    own_rows, pick, (((1,), (1,)), ((), ())), preferred_element_type=F32
                ).astype(BF16)
            token = tuple(weights.values())
        cols = GROUPS[g][0] * eighth
        start = starts[g]
        columns = slice(start, start + cols)
        if step == 0:
            size = rank // 2
            factor, grads = after(token, (inverse, out_grads))
            if order not in projected:
                turned = lax.dot_general(
                    picks[order].astype(F32),
                    factor,
                    (((1,), (0,)), ((), ())),
                    precision=lax.Precision.HIGH,
                    preferred_element_type=F32,
                )
                projected[order] = lax.dot_general(
                    turned,
                    mixed,
                    (((1,), (1,)), ((), ())),
                    precision=lax.Precision.HIGH,
                    preferred_element_type=F32,
                ).astype(BF16)
            left = projected[order]
            outgoing = jnp.dot(
                left[size:], grads[:, columns], preferred_element_type=F32
            ).astype(BF16)
            kept[g] = jnp.dot(left[:size], grads[:, columns], preferred_element_type=F32)
            bit = order[0]
        elif step < bits:
            total, piece = after(token, (kept[g], arriving[g]))
            total = total + piece.astype(F32)
            size = total.shape[0] // 2
            outgoing = total[size:].astype(BF16)
            kept[g] = total[:size]
            bit = order[step]
        elif step == bits:
            total, piece = after(token, (kept[g], arriving[g]))
            grad_low = total + piece.astype(F32)
            first = BETA_ONE * first_moment[:, columns] + (1.0 - BETA_ONE) * grad_low
            second = (
                BETA_TWO * second_moment[:, columns]
                + (1.0 - BETA_TWO) * grad_low * grad_low
            )
            outgoing = (
                first / CORRECT_ONE / (jnp.sqrt(second / CORRECT_TWO) + EPSILON)
            ).astype(BF16)
            first_parts[g], second_parts[g] = first, second
            kept[g] = outgoing
            bit = order[bits - 1]
        elif step < last:
            mine, piece = after(token, (kept[g], arriving[g]))
            outgoing = kept[g] = jnp.concatenate([mine, piece])
            bit = order[last - 1 - step]
        else:
            pieces = after(token, (kept[g], arriving[g]))
            update = update_columns(
                weights[order], pieces, update, start, width, update_scale
            )
            continue
        arriving[g] = flip(outgoing, devices, bit)
        token = outgoing
    return (
        update,
        jnp.concatenate(first_parts, axis=1),
        jnp.concatenate(second_parts, axis=1),
    )


def solution(mesh):
    dims = mesh_dims(mesh.shape["dp"])
    return jax.shard_map(
        functools.partial(local, dims),
        mesh=mesh,
        in_specs=(
            P("dp", "tensor"),
            P("dp", "tensor"),
            P("dp", None),
            P("dp", "tensor"),
            P("dp", "tensor"),
        ),
        out_specs=(P("dp", "tensor"), P("dp", "tensor"), P("dp", "tensor")),
        check_vma=False,
    )
```

```python
import functools
import itertools
import math

import jax
import jax.numpy as jnp
from jax import lax
from jax.experimental import pallas as pl
from jax.experimental.pallas import tpu as pltpu
from jax.sharding import PartitionSpec as P

BETA_ONE = 0.9
BETA_TWO = 0.999
CORRECT_ONE = 0.9999999993
CORRECT_TWO = 0.18135117
EPSILON = 1e-08

HIGHEST = lax.Precision.HIGHEST
F32 = jnp.float32
BF16 = jnp.bfloat16
BLOCK = 128
PIVOTS = 8
VMEM_LIMIT = 40 << 20

GROUPS = ((2, (0, 1, 2, 3)), (2, (2, 3, 1, 0)), (2, (1, 2, 0, 3)), (2, (0, 1, 2, 3)))
STEPS = ((0, 0), (1, 0), (2, 0), (3, 0), (0, 1), (1, 1), (2, 1), (0, 2), (3, 1), (1, 2), (2, 2), (0, 3), (3, 2), (1, 3), (2, 3), (0, 4), (3, 3), (1, 4), (2, 4), (0, 5), (1, 5), (3, 4), (2, 5), (0, 6), (1, 6), (3, 5), (2, 6), (0, 7), (3, 6), (1, 7), (2, 7), (3, 7), (0, 8), (1, 8), (2, 8), (3, 8))


GATHER = ((3, (0, 1, 2, 3)), (3, (1, 0, 2, 3)), (2, (2, 0, 1, 3)))


def flip_pairs(devices, bit):
    return [(at, at ^ (1 << bit)) for at in range(devices)]


def flip(value, devices, bit):
    return lax.ppermute(value, "dp", flip_pairs(devices, bit))


def mesh_dims(devices):
    if devices == 16:
        return (4, 2, 2)
    if devices == 64:
        return (4, 4, 4)
    return (devices, 1, 1)


def shift_pairs(dims, shift):
    pairs = []
    for place in itertools.product(*(range(size) for size in dims)):
        target = [(at + by) % size for at, by, size in zip(place, shift, dims)]
        pairs.append((flat(place, dims), flat(target, dims)))
    return pairs


def flat(place, dims):
    index = 0
    for at, size in zip(place, dims):
        index = index * size + at
    return index


def send(value, dims, shift):
    return lax.ppermute(value, "dp", shift_pairs(dims, shift))


def dot_nn(a, b):
    return lax.dot_general(
        a, b, (((1,), (0,)), ((), ())), precision=HIGHEST, preferred_element_type=F32
    )


def dot_nt(a, b):
    return lax.dot_general(
        a, b, (((1,), (1,)), ((), ())), precision=HIGHEST, preferred_element_type=F32
    )


def inverse_factor(block):
    size = block.shape[0]
    tiles = size // 8
    lane = lax.broadcasted_iota(jnp.int32, (8, size), 1)
    sub = lax.broadcasted_iota(jnp.int32, (8, size), 0)
    spread = lambda value: jnp.broadcast_to(value, (8, size))
    work = [block[8 * i : 8 * i + 8, :] for i in range(tiles)]
    scale = [jnp.zeros((8, size), F32) for _ in range(tiles)]
    for base in range(0, size, PIVOTS):
        first = base // 8
        cols = {
            (i, k): spread(work[i][:, base + k : base + k + 1])
            for i in range(first, tiles)
            for k in range(PIVOTS)
        }
        for k in range(PIVOTS):
            j = base + k
            r, q = j % 8, j // 8
            pivot = spread(cols[q, k][r : r + 1, :])
            recip = 1.0 / pivot
            row = jnp.where(lane == j, 1.0, spread(work[q][r : r + 1, :]))
            later = {m: spread(cols[q, m][r : r + 1, :]) for m in range(k + 1, PIVOTS)}
            scale[q] = jnp.where(sub == r, pivot, scale[q])
            for i in range(q, tiles):
                ratio = cols[i, k] * recip
                cleared = lane == j
                if i == q:
                    ratio = jnp.where(sub > r, ratio, 0.0)
                    cleared = cleared & (sub > r)
                for m in range(k + 1, PIVOTS):
                    cols[i, m] = cols[i, m] - ratio * later[m]
                work[i] = jnp.where(cleared, 0.0, work[i]) - ratio * row
    out = []
    for i in range(tiles):
        at = sub + 8 * i
        lower = jnp.where(lane == at, 1.0, jnp.where(lane < at, work[i], 0.0))
        out.append(lower * lax.rsqrt(scale[i]))
    return jnp.concatenate(out, axis=0)


def lower_blocks(size):
    return [(i, j) for i in range(size // BLOCK) for j in range(i + 1)]


def factor_steps(first, last, work_ref, out_ref):
    size = out_ref.shape[0]

    def step(at, carry):
        base = pl.multiple_of(at * BLOCK, BLOCK)
        inverse = inverse_factor(work_ref[pl.ds(base, BLOCK), pl.ds(base, BLOCK)])
        rows = dot_nn(inverse, out_ref[pl.ds(base, BLOCK), :])
        out_ref[pl.ds(base, BLOCK), :] = rows

        @pl.when(at < size // BLOCK - 1)
        def _():
            panel = dot_nt(work_ref[:, pl.ds(base, BLOCK)], inverse)
            below = lax.broadcasted_iota(jnp.int32, (size, BLOCK), 0) >= base + BLOCK
            panel = jnp.where(below, panel, 0.0)
            work_ref[...] -= dot_nt(panel, panel)
            out_ref[...] -= dot_nn(panel, rows)

        return carry

    lax.fori_loop(first, last, step, 0)


def factor_head(blocks, steps, packed_ref, work_ref, out_ref):
    size = out_ref.shape[0]
    work_ref[...] = jnp.zeros_like(work_ref)
    for at, (i, j) in enumerate(blocks):
        work_ref[i * BLOCK : (i + 1) * BLOCK, j * BLOCK : (j + 1) * BLOCK] = packed_ref[
            at * BLOCK : (at + 1) * BLOCK, :
        ]
    out_ref[...] = jnp.where(
        lax.broadcasted_iota(jnp.int32, (size, size), 0)
        == lax.broadcasted_iota(jnp.int32, (size, size), 1),
        1.0,
        0.0,
    )
    factor_steps(0, steps, work_ref, out_ref)


def factor_rest(steps, start_ref, done_ref, out_ref, work_ref):
    work_ref[...] = start_ref[...]
    out_ref[...] = done_ref[...]
    factor_steps(steps, out_ref.shape[0] // BLOCK, work_ref, out_ref)


def head_of_factor(packed, blocks, size, steps):
    square = jax.ShapeDtypeStruct((size, size), F32)
    return pl.pallas_call(
        functools.partial(factor_head, blocks, steps),
        out_shape=(square, square),
        in_specs=[pl.BlockSpec(memory_space=pltpu.VMEM)],
        out_specs=(pl.BlockSpec(memory_space=pltpu.VMEM),) * 2,
        compiler_params=pltpu.CompilerParams(vmem_limit_bytes=VMEM_LIMIT),
        name="factor_head",
    )(packed)


def rest_of_factor(work, done, steps):
    return pl.pallas_call(
        functools.partial(factor_rest, steps),
        out_shape=jax.ShapeDtypeStruct(work.shape, F32),
        in_specs=[pl.BlockSpec(memory_space=pltpu.VMEM)] * 2,
        out_specs=pl.BlockSpec(memory_space=pltpu.VMEM),
        scratch_shapes=[pltpu.VMEM(work.shape, F32)],
        compiler_params=pltpu.CompilerParams(vmem_limit_bytes=VMEM_LIMIT),
        name="factor_rest",
    )(work, done)


def gram_and_sketch(sketch, half, dims, own, core):
    devices = math.prod(dims)
    bits = devices.bit_length() - 1
    size = sketch.shape[1]
    blocks = lower_blocks(size)
    split = len(blocks) // 2
    gram = jnp.dot(sketch.T, sketch, precision=HIGHEST, preferred_element_type=F32)
    tiles = [
        gram[i * BLOCK : (i + 1) * BLOCK, j * BLOCK : (j + 1) * BLOCK] for i, j in blocks
    ]
    mine = jnp.where(
        core == 0, jnp.concatenate(tiles[:split]), jnp.concatenate(tiles[split:])
    )
    plane = dims[1] * dims[2]
    share = mine.shape[0] // plane
    at_of = lambda a, b: ((own[1] + a) % dims[1] * dims[2] + (own[2] + b) % dims[2]) * share
    shifts = list(itertools.product(range(dims[1]), range(dims[2])))
    part = lambda a, b: lax.dynamic_slice_in_dim(mine, at_of(a, b), share, 0)
    outgoing = [part(a, b) for a, b in shifts[1:]]
    total = part(0, 0)
    arrived = [send(piece, dims, (0, a, b)) for (a, b), piece in zip(shifts[1:], outgoing)]

    groups = gather_groups(half.shape[0], bits)
    (half,) = after(outgoing[-1], (half,))
    parts = [(groups, half[None], flip(half[None], devices, groups[0][1][-1]))]

    def widen(stage, token, chosen=slice(None)):
        split = []
        for members, rows, piece in parts[chosen]:
            rows, piece = after(token, (rows, piece))
            token = jnp.concatenate([rows, piece])
            start = 0
            for bit, same in itertools.groupby(members, lambda m: m[1][-1 - stage]):
                same = list(same)
                tall = sum(rows for rows, _ in same)
                piece = token[:, start : start + tall]
                start += tall
                split.append((same, piece, flip(piece, devices, bit)))
        parts[chosen] = split
        return token

    arrived = after(half, arrived)
    for piece in arrived:
        total = total + piece
    arrived = [send(total, dims, (by, 0, 0)) for by in range(1, dims[0])]
    token = widen(1, arrived[0])
    arrived = after(token, arrived)
    places = jnp.stack([total, *arrived])
    order = [(own[0] - z) % dims[0] for z in range(dims[0])]
    total = functools.reduce(
        jnp.add, [lax.dynamic_index_in_dim(places, at, 0, keepdims=False) for at in order]
    )
    arrived = [send(total, dims, (0, -a, -b)) for a, b in shifts[1:]]
    token = widen(2, arrived[0], slice(0, max(1, len(parts) - 1)))
    arrived = after(token, arrived)
    whole = lax.dynamic_update_slice_in_dim(
        jnp.zeros_like(mine), total, at_of(0, 0), 0
    )
    for (a, b), piece in zip(shifts[1:], arrived):
        whole = lax.dynamic_update_slice_in_dim(whole, piece, at_of(a, b), 0)
    other = lax.ppermute(whole, "tensor", [(0, 1), (1, 0)])
    token = whole
    if len(parts) > 2:
        token = widen(2, token, slice(-1, None))
    for stage in range(3, bits - 1):
        token = widen(stage, token)
    whole, other = after(token, (whole, other))
    packed = jnp.where(
        core == 0, jnp.concatenate([whole, other]), jnp.concatenate([other, whole])
    )
    work, done = head_of_factor(packed, blocks, size, 1)
    token = widen(bits - 1, work)
    work, done = after(token, (work, done))
    inverse = rest_of_factor(work, done, 1)
    orders = [order for _, order in groups]
    return inverse, orders, [part[1] for part in parts], [part[2] for part in parts]


def gather_groups(rows, bits):
    chosen = GATHER if rows >= 4 * BLOCK else ((8, GATHER[0][1]),)
    return [(share * rows // 8, order + tuple(range(4, bits))) for share, order in chosen]


def mix_kernel(groups, limit, table_ref, left_ref, right_ref, *refs):
    at = pl.program_id(0)
    out_ref = refs[-1]
    total = None
    for side, source in enumerate((left_ref, right_ref)):
        rows = []
        for g in range(groups):
            near, far = refs[2 * g], refs[2 * g + 1]
            place = table_ref[side, g, at]
            far_place = lax.rem(place, limit)
            rows.append(jnp.where(place < limit, near[far_place], far[far_place]))
        term = jnp.dot(
            source[...], jnp.concatenate(rows, axis=0), preferred_element_type=F32
        )
        total = term if total is None else total + term

    @pl.when(at == 0)
    def _():
        out_ref[...] = total

    @pl.when(at > 0)
    def _():
        out_ref[...] += total


def mix(left, right, near, far, groups, dp, core):
    limit, _, cols = near[0].shape
    bits = limit.bit_length()
    count = len(groups)
    blocks = jnp.arange(limit, dtype=jnp.int32)
    table = []
    for side in (core, 1 - core):
        apart = (side * limit + blocks) ^ dp
        row = []
        for order in groups:
            place = jnp.zeros_like(apart)
            for bit in order:
                place = place * 2 + ((apart >> bit) & 1)
            row.append(place)
        table.append(jnp.stack(row))
    table = jnp.stack(table)
    block = left.shape[1] // limit
    in_specs = [pl.BlockSpec((left.shape[0], block), lambda i, t: (0, i))] * 2
    operands = [left, right]
    for g in range(count):
        spec = pl.BlockSpec(near[g].shape, lambda i, t: (0, 0, 0))
        in_specs += [spec, spec]
        operands += [near[g], far[g]]
    return pl.pallas_call(
        functools.partial(mix_kernel, count, limit),
        grid_spec=pltpu.PrefetchScalarGridSpec(
            num_scalar_prefetch=1,
            grid=(limit,),
            in_specs=in_specs,
            out_specs=pl.BlockSpec((left.shape[0], cols), lambda i, t: (0, 0)),
        ),
        out_shape=jax.ShapeDtypeStruct((left.shape[0], cols), F32),
        compiler_params=pltpu.CompilerParams(vmem_limit_bytes=VMEM_LIMIT),
        name="mix",
    )(table, *operands)


def update_kernel(scale, count, *refs):
    weight_ref, pieces, out_ref = refs[0], refs[1 : 1 + count], refs[-1]
    rows = pieces[0].shape[0]
    total = None
    for at, piece in enumerate(pieces):
        term = jnp.dot(
            weight_ref[:, at * rows : (at + 1) * rows],
            piece[...],
            preferred_element_type=F32,
        )
        total = term if total is None else total + term
    out_ref[...] = scale * total


def update_columns(weight, pieces, previous, start, width, scale):
    tall, rank = weight.shape
    rows, cols = pieces[0].shape
    wide = min(1024, cols)
    first = start // wide
    in_specs = [pl.BlockSpec((tall, rank), lambda j: (0, 0))]
    in_specs += [pl.BlockSpec((rows, wide), lambda j: (0, j)) for _ in pieces]
    operands = [weight, *pieces]
    aliases = {}
    if previous is not None:
        aliases = {len(operands): 0}
        in_specs.append(pl.BlockSpec(memory_space=pl.ANY))
        operands.append(previous)
    return pl.pallas_call(
        functools.partial(update_kernel, scale, len(pieces)),
        grid=(cols // wide,),
        out_shape=jax.ShapeDtypeStruct((tall, width), F32),
        in_specs=in_specs,
        out_specs=pl.BlockSpec((tall, wide), lambda j: (0, first + j)),
        input_output_aliases=aliases,
        compiler_params=pltpu.CompilerParams(vmem_limit_bytes=VMEM_LIMIT),
        name="update_columns",
    )(*operands)


def selection(devices, dp, order, rank):
    index = jnp.zeros((), jnp.int32)
    for bit in order:
        index = index[..., None] | jnp.array([0, 1 << bit], jnp.int32)
    piece = rank // devices
    index = (index ^ dp)[..., None] * piece + jnp.arange(piece, dtype=jnp.int32)
    index = index.reshape(rank)
    return (index[:, None] == jnp.arange(rank, dtype=jnp.int32)[None, :]).astype(BF16)


def after(token, values):
    if token is None:
        return values
    return lax.optimization_barrier((*values, token))[:-1]


def local(dims, activations, out_grads, sketch, first_moment, second_moment):
    devices = math.prod(dims)
    bits = devices.bit_length() - 1
    dp = lax.axis_index("dp")
    core = lax.axis_index("tensor")
    own = (dp // (dims[1] * dims[2]), dp // dims[2] % dims[1], dp % dims[2])
    rank = sketch.shape[1]
    width = out_grads.shape[1]
    depth = activations.shape[1] * 2

    beside = lax.ppermute(activations, "tensor", [(0, 1), (1, 0)])
    half = lax.dynamic_slice_in_dim(sketch, core * (rank // 2), rank // 2, 1).astype(BF16)
    inverse, groups, near, far = gram_and_sketch(sketch, half, dims, own, core)
    *far, activations = after(inverse, (*far, activations))
    mixed_half = mix(activations, beside, near, far, groups, dp, core)
    mixed_other = lax.ppermute(mixed_half, "tensor", [(0, 1), (1, 0)])
    mixed = jnp.where(
        core == 0,
        jnp.concatenate([mixed_half, mixed_other], axis=1),
        jnp.concatenate([mixed_other, mixed_half], axis=1),
    )

    orders = [order + tuple(range(4, bits)) for _, order in GROUPS]
    picks = {order: selection(devices, dp, order, rank) for order in orders}
    projected, weights = {}, {}
    update_scale = math.sqrt(depth / rank)
    eighth = width // 8
    starts = [sum(share for share, _ in GROUPS[:g]) * eighth for g in range(len(GROUPS))]
    kept = [None] * len(GROUPS)
    arriving = [None] * len(GROUPS)
    first_parts = [None] * len(GROUPS)
    second_parts = [None] * len(GROUPS)
    token = None
    update = None
    last = 2 * bits
    steps = STEPS if STEPS and bits == 4 else [
        (g, s) for s in range(last + 1) for g in range(len(GROUPS))
    ]
    for g, step in steps:
        order = orders[g]
        if step == 1 and not weights:
            rows, factor = after(token, (sketch, inverse))
            own_rows = dot_nt(rows, factor).astype(BF16)
            for each, pick in picks.items():
                weights[each] = lax.dot_general(
                    own_rows, pick, (((1,), (1,)), ((), ())), preferred_element_type=F32
                ).astype(BF16)
            token = tuple(weights.values())
        cols = GROUPS[g][0] * eighth
        start = starts[g]
        columns = slice(start, start + cols)
        if step == 0:
            size = rank // 2
            (grads,) = after(token, (out_grads,))
            if not projected:
                turned = lax.dot_general(
                    picks[order].astype(F32),
                    inverse,
                    (((1,), (0,)), ((), ())),
                    precision=lax.Precision.HIGH,
                    preferred_element_type=F32,
                )
                projected[order] = lax.dot_general(
                    turned,
                    mixed,
                    (((1,), (1,)), ((), ())),
                    precision=lax.Precision.HIGH,
                    preferred_element_type=F32,
                ).astype(BF16)
            elif order not in projected:
                base, rows = next(iter(projected.items()))
                (rows,) = after(token, (rows,))
                bare = rows.reshape((2,) * bits + (rank // devices, rows.shape[1]))
                axes = [base.index(bit) for bit in order] + [bits, bits + 1]
                projected[order] = bare.transpose(axes).reshape(rows.shape)
            left = projected[order]
            outgoing = jnp.dot(
                left[size:], grads[:, columns], preferred_element_type=F32
            ).astype(BF16)
            grads, left, outgoing = lax.optimization_barrier((grads, left, outgoing))
            kept[g] = jnp.dot(left[:size], grads[:, columns], preferred_element_type=F32)
            bit = order[0]
        elif step < bits:
            total, piece = after(token, (kept[g], arriving[g]))
            total = total + piece.astype(F32)
            size = total.shape[0] // 2
            outgoing = total[size:].astype(BF16)
            kept[g] = total[:size]
            bit = order[step]
        elif step == bits:
            total, piece = after(token, (kept[g], arriving[g]))
            grad_low = total + piece.astype(F32)
            first = BETA_ONE * first_moment[:, columns] + (1.0 - BETA_ONE) * grad_low
            second = (
                BETA_TWO * second_moment[:, columns]
                + (1.0 - BETA_TWO) * grad_low * grad_low
            )
            outgoing = (
                first / CORRECT_ONE / (jnp.sqrt(second / CORRECT_TWO) + EPSILON)
            ).astype(BF16)
            first_parts[g], second_parts[g] = first, second
            kept[g] = outgoing
            bit = order[bits - 1]
        elif step < last:
            mine, piece = after(token, (kept[g], arriving[g]))
            outgoing = kept[g] = jnp.concatenate([mine, piece])
            bit = order[last - 1 - step]
        else:
            pieces = after(token, (kept[g], arriving[g]))
            update = update_columns(
                weights[order], pieces, update, start, width, update_scale
            )
            continue
        arriving[g] = flip(outgoing, devices, bit)
        token = outgoing
    return (
        update,
        jnp.concatenate(first_parts, axis=1),
        jnp.concatenate(second_parts, axis=1),
    )


def solution(mesh):
    dims = mesh_dims(mesh.shape["dp"])
    return jax.shard_map(
        functools.partial(local, dims),
        mesh=mesh,
        in_specs=(
            P("dp", "tensor"),
            P("dp", "tensor"),
            P("dp", None),
            P("dp", "tensor"),
            P("dp", "tensor"),
        ),
        out_specs=(P("dp", "tensor"), P("dp", "tensor"), P("dp", "tensor")),
        check_vma=False,
    )
```

```python
import functools
import itertools
import math

import jax
import jax.numpy as jnp
from jax import lax
from jax.experimental import pallas as pl
from jax.experimental.pallas import tpu as pltpu
from jax.sharding import PartitionSpec as P

BETA_ONE = 0.9
BETA_TWO = 0.999
CORRECT_ONE = 0.9999999993
CORRECT_TWO = 0.18135117
EPSILON = 1e-08

HIGHEST = lax.Precision.HIGHEST
F32 = jnp.float32
BF16 = jnp.bfloat16
BLOCK = 128
PIVOTS = 8
VMEM_LIMIT = 40 << 20

GROUPS = ((2, (2, 1, 0, 3)), (2, (1, 0, 2, 3)), (2, (0, 1, 2, 3)), (2, (2, 0, 1, 3)))
STEPS = ((0, 0), (1, 0), (2, 0), (3, 0), (0, 1), (1, 1), (2, 1), (0, 2), (1, 2), (3, 1), (0, 3), (2, 2), (1, 3), (0, 4), (2, 3), (3, 2), (1, 4), (3, 3), (0, 5), (2, 4), (0, 6), (1, 5), (3, 4), (2, 5), (0, 7), (1, 6), (3, 5), (2, 6), (3, 6), (1, 7), (2, 7), (3, 7), (0, 8), (1, 8), (2, 8), (3, 8))


GATHER = ((3, (0, 1, 2, 3)), (3, (1, 0, 2, 3)), (2, (2, 1, 0, 3)))


def flip_pairs(devices, bit):
    return [(at, at ^ (1 << bit)) for at in range(devices)]


def flip(value, devices, bit):
    return lax.ppermute(value, "dp", flip_pairs(devices, bit))


def mesh_dims(devices):
    if devices == 16:
        return (4, 2, 2)
    if devices == 64:
        return (4, 4, 4)
    return (devices, 1, 1)


def shift_pairs(dims, shift):
    pairs = []
    for place in itertools.product(*(range(size) for size in dims)):
        target = [(at + by) % size for at, by, size in zip(place, shift, dims)]
        pairs.append((flat(place, dims), flat(target, dims)))
    return pairs


def flat(place, dims):
    index = 0
    for at, size in zip(place, dims):
        index = index * size + at
    return index


def send(value, dims, shift):
    return lax.ppermute(value, "dp", shift_pairs(dims, shift))


def dot_nn(a, b):
    return lax.dot_general(
        a, b, (((1,), (0,)), ((), ())), precision=HIGHEST, preferred_element_type=F32
    )


def dot_nt(a, b):
    return lax.dot_general(
        a, b, (((1,), (1,)), ((), ())), precision=HIGHEST, preferred_element_type=F32
    )


def inverse_factor(block):
    size = block.shape[0]
    tiles = size // 8
    lane = lax.broadcasted_iota(jnp.int32, (8, size), 1)
    sub = lax.broadcasted_iota(jnp.int32, (8, size), 0)
    spread = lambda value: jnp.broadcast_to(value, (8, size))
    work = [block[8 * i : 8 * i + 8, :] for i in range(tiles)]
    scale = [jnp.zeros((8, size), F32) for _ in range(tiles)]
    for base in range(0, size, PIVOTS):
        first = base // 8
        cols = {
            (i, k): spread(work[i][:, base + k : base + k + 1])
            for i in range(first, tiles)
            for k in range(PIVOTS)
        }
        for k in range(PIVOTS):
            j = base + k
            r, q = j % 8, j // 8
            pivot = spread(cols[q, k][r : r + 1, :])
            recip = 1.0 / pivot
            row = jnp.where(lane == j, 1.0, spread(work[q][r : r + 1, :]))
            later = {m: spread(cols[q, m][r : r + 1, :]) for m in range(k + 1, PIVOTS)}
            scale[q] = jnp.where(sub == r, pivot, scale[q])
            for i in range(q, tiles):
                ratio = cols[i, k] * recip
                cleared = lane == j
                if i == q:
                    ratio = jnp.where(sub > r, ratio, 0.0)
                    cleared = cleared & (sub > r)
                for m in range(k + 1, PIVOTS):
                    cols[i, m] = cols[i, m] - ratio * later[m]
                work[i] = jnp.where(cleared, 0.0, work[i]) - ratio * row
    out = []
    for i in range(tiles):
        at = sub + 8 * i
        lower = jnp.where(lane == at, 1.0, jnp.where(lane < at, work[i], 0.0))
        out.append(lower * lax.rsqrt(scale[i]))
    return jnp.concatenate(out, axis=0)


def lower_blocks(size):
    return [(i, j) for i in range(size // BLOCK) for j in range(i + 1)]


def factor_steps(first, last, work_ref, out_ref):
    size = out_ref.shape[0]

    def step(at, carry):
        base = pl.multiple_of(at * BLOCK, BLOCK)
        inverse = inverse_factor(work_ref[pl.ds(base, BLOCK), pl.ds(base, BLOCK)])
        rows = dot_nn(inverse, out_ref[pl.ds(base, BLOCK), :])
        out_ref[pl.ds(base, BLOCK), :] = rows

        @pl.when(at < size // BLOCK - 1)
        def _():
            panel = dot_nt(work_ref[:, pl.ds(base, BLOCK)], inverse)
            below = lax.broadcasted_iota(jnp.int32, (size, BLOCK), 0) >= base + BLOCK
            panel = jnp.where(below, panel, 0.0)
            work_ref[...] -= dot_nt(panel, panel)
            out_ref[...] -= dot_nn(panel, rows)

        return carry

    lax.fori_loop(first, last, step, 0)


def factor_head(blocks, steps, packed_ref, work_ref, out_ref):
    size = out_ref.shape[0]
    work_ref[...] = jnp.zeros_like(work_ref)
    for at, (i, j) in enumerate(blocks):
        work_ref[i * BLOCK : (i + 1) * BLOCK, j * BLOCK : (j + 1) * BLOCK] = packed_ref[
            at * BLOCK : (at + 1) * BLOCK, :
        ]
    out_ref[...] = jnp.where(
        lax.broadcasted_iota(jnp.int32, (size, size), 0)
        == lax.broadcasted_iota(jnp.int32, (size, size), 1),
        1.0,
        0.0,
    )
    factor_steps(0, steps, work_ref, out_ref)


def factor_rest(steps, start_ref, done_ref, out_ref, work_ref):
    work_ref[...] = start_ref[...]
    out_ref[...] = done_ref[...]
    factor_steps(steps, out_ref.shape[0] // BLOCK, work_ref, out_ref)


def head_of_factor(packed, blocks, size, steps):
    square = jax.ShapeDtypeStruct((size, size), F32)
    return pl.pallas_call(
        functools.partial(factor_head, blocks, steps),
        out_shape=(square, square),
        in_specs=[pl.BlockSpec(memory_space=pltpu.VMEM)],
        out_specs=(pl.BlockSpec(memory_space=pltpu.VMEM),) * 2,
        compiler_params=pltpu.CompilerParams(vmem_limit_bytes=VMEM_LIMIT),
        name="factor_head",
    )(packed)


def rest_of_factor(work, done, steps):
    return pl.pallas_call(
        functools.partial(factor_rest, steps),
        out_shape=jax.ShapeDtypeStruct(work.shape, F32),
        in_specs=[pl.BlockSpec(memory_space=pltpu.VMEM)] * 2,
        out_specs=pl.BlockSpec(memory_space=pltpu.VMEM),
        scratch_shapes=[pltpu.VMEM(work.shape, F32)],
        compiler_params=pltpu.CompilerParams(vmem_limit_bytes=VMEM_LIMIT),
        name="factor_rest",
    )(work, done)


def gram_and_sketch(sketch, half, dims, own, core):
    devices = math.prod(dims)
    bits = devices.bit_length() - 1
    size = sketch.shape[1]
    blocks = lower_blocks(size)
    split = len(blocks) // 2
    gram = jnp.dot(sketch.T, sketch, precision=HIGHEST, preferred_element_type=F32)
    tiles = [
        gram[i * BLOCK : (i + 1) * BLOCK, j * BLOCK : (j + 1) * BLOCK] for i, j in blocks
    ]
    mine = jnp.where(
        core == 0, jnp.concatenate(tiles[:split]), jnp.concatenate(tiles[split:])
    )
    plane = dims[1] * dims[2]
    share = mine.shape[0] // plane
    at_of = lambda a, b: ((own[1] + a) % dims[1] * dims[2] + (own[2] + b) % dims[2]) * share
    shifts = list(itertools.product(range(dims[1]), range(dims[2])))
    part = lambda a, b: lax.dynamic_slice_in_dim(mine, at_of(a, b), share, 0)
    outgoing = [part(a, b) for a, b in shifts[1:]]
    total = part(0, 0)
    arrived = [send(piece, dims, (0, a, b)) for (a, b), piece in zip(shifts[1:], outgoing)]

    groups = gather_groups(half.shape[0], bits)
    (half,) = after(outgoing[-1], (half,))
    parts = [(groups, half[None], flip(half[None], devices, groups[0][1][-1]))]

    def widen(stage, token, chosen=slice(None)):
        split = []
        for members, rows, piece in parts[chosen]:
            rows, piece = after(token, (rows, piece))
            token = jnp.concatenate([rows, piece])
            start = 0
            for bit, same in itertools.groupby(members, lambda m: m[1][-1 - stage]):
                same = list(same)
                tall = sum(rows for rows, _ in same)
                piece = token[:, start : start + tall]
                start += tall
                split.append((same, piece, flip(piece, devices, bit)))
        parts[chosen] = split
        return token

    arrived = after(half, arrived)
    for piece in arrived:
        total = total + piece
    arrived = [send(total, dims, (by, 0, 0)) for by in range(1, dims[0])]
    token = widen(1, arrived[0])
    arrived = after(token, arrived)
    places = jnp.stack([total, *arrived])
    order = [(own[0] - z) % dims[0] for z in range(dims[0])]
    total = functools.reduce(
        jnp.add, [lax.dynamic_index_in_dim(places, at, 0, keepdims=False) for at in order]
    )
    arrived = [send(total, dims, (0, -a, -b)) for a, b in shifts[1:]]
    token = widen(2, arrived[0], slice(0, max(1, len(parts) - 1)))
    arrived = after(token, arrived)
    whole = lax.dynamic_update_slice_in_dim(
        jnp.zeros_like(mine), total, at_of(0, 0), 0
    )
    for (a, b), piece in zip(shifts[1:], arrived):
        whole = lax.dynamic_update_slice_in_dim(whole, piece, at_of(a, b), 0)
    other = lax.ppermute(whole, "tensor", [(0, 1), (1, 0)])
    token = whole
    if len(parts) > 2:
        token = widen(2, token, slice(-1, None))
    for stage in range(3, bits - 1):
        token = widen(stage, token)
    whole, other = after(token, (whole, other))
    packed = jnp.where(
        core == 0, jnp.concatenate([whole, other]), jnp.concatenate([other, whole])
    )
    work, done = head_of_factor(packed, blocks, size, 1)
    token = widen(bits - 1, work)
    work, done = after(token, (work, done))
    inverse = rest_of_factor(work, done, 1)
    orders = [order for _, order in groups]
    return inverse, orders, [part[1] for part in parts], [part[2] for part in parts]


def gather_groups(rows, bits):
    chosen = GATHER if rows >= 4 * BLOCK else ((8, GATHER[0][1]),)
    return [(share * rows // 8, order + tuple(range(4, bits))) for share, order in chosen]


def mix_kernel(groups, limit, table_ref, left_ref, right_ref, *refs):
    at = pl.program_id(0)
    out_ref = refs[-1]
    total = None
    for side, source in enumerate((left_ref, right_ref)):
        rows = []
        for g in range(groups):
            near, far = refs[2 * g], refs[2 * g + 1]
            place = table_ref[side, g, at]
            far_place = lax.rem(place, limit)
            rows.append(jnp.where(place < limit, near[far_place], far[far_place]))
        term = jnp.dot(
            source[...], jnp.concatenate(rows, axis=0), preferred_element_type=F32
        )
        total = term if total is None else total + term

    @pl.when(at == 0)
    def _():
        out_ref[...] = total

    @pl.when(at > 0)
    def _():
        out_ref[...] += total


def mix(left, right, near, far, groups, dp, core):
    limit, _, cols = near[0].shape
    bits = limit.bit_length()
    count = len(groups)
    blocks = jnp.arange(limit, dtype=jnp.int32)
    table = []
    for side in (core, 1 - core):
        apart = (side * limit + blocks) ^ dp
        row = []
        for order in groups:
            place = jnp.zeros_like(apart)
            for bit in order:
                place = place * 2 + ((apart >> bit) & 1)
            row.append(place)
        table.append(jnp.stack(row))
    table = jnp.stack(table)
    block = left.shape[1] // limit
    in_specs = [pl.BlockSpec((left.shape[0], block), lambda i, t: (0, i))] * 2
    operands = [left, right]
    for g in range(count):
        spec = pl.BlockSpec(near[g].shape, lambda i, t: (0, 0, 0))
        in_specs += [spec, spec]
        operands += [near[g], far[g]]
    return pl.pallas_call(
        functools.partial(mix_kernel, count, limit),
        grid_spec=pltpu.PrefetchScalarGridSpec(
            num_scalar_prefetch=1,
            grid=(limit,),
            in_specs=in_specs,
            out_specs=pl.BlockSpec((left.shape[0], cols), lambda i, t: (0, 0)),
        ),
        out_shape=jax.ShapeDtypeStruct((left.shape[0], cols), F32),
        compiler_params=pltpu.CompilerParams(vmem_limit_bytes=VMEM_LIMIT),
        name="mix",
    )(table, *operands)


def update_kernel(scale, count, *refs):
    weight_ref, pieces, out_ref = refs[0], refs[1 : 1 + count], refs[-1]
    rows = pieces[0].shape[0]
    total = None
    for at, piece in enumerate(pieces):
        term = jnp.dot(
            weight_ref[:, at * rows : (at + 1) * rows],
            piece[...],
            preferred_element_type=F32,
        )
        total = term if total is None else total + term
    out_ref[...] = scale * total


def update_columns(weight, pieces, previous, start, width, scale):
    tall, rank = weight.shape
    rows, cols = pieces[0].shape
    wide = min(1024, cols)
    first = start // wide
    in_specs = [pl.BlockSpec((tall, rank), lambda j: (0, 0))]
    in_specs += [pl.BlockSpec((rows, wide), lambda j: (0, j)) for _ in pieces]
    operands = [weight, *pieces]
    aliases = {}
    if previous is not None:
        aliases = {len(operands): 0}
        in_specs.append(pl.BlockSpec(memory_space=pl.ANY))
        operands.append(previous)
    return pl.pallas_call(
        functools.partial(update_kernel, scale, len(pieces)),
        grid=(cols // wide,),
        out_shape=jax.ShapeDtypeStruct((tall, width), F32),
        in_specs=in_specs,
        out_specs=pl.BlockSpec((tall, wide), lambda j: (0, first + j)),
        input_output_aliases=aliases,
        compiler_params=pltpu.CompilerParams(vmem_limit_bytes=VMEM_LIMIT),
        name="update_columns",
    )(*operands)


def selection(devices, dp, order, rank):
    index = jnp.zeros((), jnp.int32)
    for bit in order:
        index = index[..., None] | jnp.array([0, 1 << bit], jnp.int32)
    piece = rank // devices
    index = (index ^ dp)[..., None] * piece + jnp.arange(piece, dtype=jnp.int32)
    index = index.reshape(rank)
    return (index[:, None] == jnp.arange(rank, dtype=jnp.int32)[None, :]).astype(BF16)


def after(token, values):
    if token is None:
        return values
    return lax.optimization_barrier((*values, token))[:-1]


def local(dims, activations, out_grads, sketch, first_moment, second_moment):
    devices = math.prod(dims)
    bits = devices.bit_length() - 1
    dp = lax.axis_index("dp")
    core = lax.axis_index("tensor")
    own = (dp // (dims[1] * dims[2]), dp // dims[2] % dims[1], dp % dims[2])
    rank = sketch.shape[1]
    width = out_grads.shape[1]
    depth = activations.shape[1] * 2

    beside = lax.ppermute(activations, "tensor", [(0, 1), (1, 0)])
    half = lax.dynamic_slice_in_dim(sketch, core * (rank // 2), rank // 2, 1).astype(BF16)
    inverse, groups, near, far = gram_and_sketch(sketch, half, dims, own, core)
    *far, activations = after(inverse, (*far, activations))
    mixed_half = mix(activations, beside, near, far, groups, dp, core)
    mixed_other = lax.ppermute(mixed_half, "tensor", [(0, 1), (1, 0)])
    mixed = jnp.where(
        core == 0,
        jnp.concatenate([mixed_half, mixed_other], axis=1),
        jnp.concatenate([mixed_other, mixed_half], axis=1),
    )

    orders = [order + tuple(range(4, bits)) for _, order in GROUPS]
    picks = {order: selection(devices, dp, order, rank) for order in orders}
    projected, weights = {}, {}
    update_scale = math.sqrt(depth / rank)
    eighth = width // 8
    starts = [sum(share for share, _ in GROUPS[:g]) * eighth for g in range(len(GROUPS))]
    kept = [None] * len(GROUPS)
    arriving = [None] * len(GROUPS)
    first_parts = [None] * len(GROUPS)
    second_parts = [None] * len(GROUPS)
    token = None
    update = None
    last = 2 * bits
    steps = STEPS if STEPS and bits == 4 else [
        (g, s) for s in range(last + 1) for g in range(len(GROUPS))
    ]
    for g, step in steps:
        order = orders[g]
        if step == 1 and not weights:
            rows, factor = after(token, (sketch, inverse))
            own_rows = dot_nt(rows, factor).astype(BF16)
            for each, pick in picks.items():
                weights[each] = lax.dot_general(
                    own_rows, pick, (((1,), (1,)), ((), ())), preferred_element_type=F32
                ).astype(BF16)
            token = tuple(weights.values())
        cols = GROUPS[g][0] * eighth
        start = starts[g]
        columns = slice(start, start + cols)
        if step == 0:
            size = rank // 2
            (grads,) = after(token, (out_grads,))
            if not projected:
                turned = lax.dot_general(
                    picks[order].astype(F32),
                    inverse,
                    (((1,), (0,)), ((), ())),
                    precision=lax.Precision.HIGH,
                    preferred_element_type=F32,
                )
                projected[order] = lax.dot_general(
                    turned,
                    mixed,
                    (((1,), (1,)), ((), ())),
                    precision=lax.Precision.HIGH,
                    preferred_element_type=F32,
                ).astype(BF16)
            elif order not in projected:
                base, rows = next(iter(projected.items()))
                (rows,) = after(token, (rows,))
                bare = rows.reshape((2,) * bits + (rank // devices, rows.shape[1]))
                axes = [base.index(bit) for bit in order] + [bits, bits + 1]
                projected[order] = bare.transpose(axes).reshape(rows.shape)
            left = projected[order]
            outgoing = jnp.dot(
                left[size:], grads[:, columns], preferred_element_type=F32
            ).astype(BF16)
            grads, left, outgoing = lax.optimization_barrier((grads, left, outgoing))
            kept[g] = jnp.dot(left[:size], grads[:, columns], preferred_element_type=F32)
            bit = order[0]
        elif step < bits:
            total, piece = after(token, (kept[g], arriving[g]))
            total = total + piece.astype(F32)
            size = total.shape[0] // 2
            outgoing = total[size:].astype(BF16)
            kept[g] = total[:size]
            bit = order[step]
        elif step == bits:
            total, piece = after(token, (kept[g], arriving[g]))
            grad_low = total + piece.astype(F32)
            first = BETA_ONE * first_moment[:, columns] + (1.0 - BETA_ONE) * grad_low
            second = (
                BETA_TWO * second_moment[:, columns]
                + (1.0 - BETA_TWO) * grad_low * grad_low
            )
            outgoing = (
                first / CORRECT_ONE / (jnp.sqrt(second / CORRECT_TWO) + EPSILON)
            ).astype(BF16)
            first_parts[g], second_parts[g] = first, second
            kept[g] = outgoing
            bit = order[bits - 1]
        elif step < last:
            mine, piece = after(token, (kept[g], arriving[g]))
            outgoing = kept[g] = jnp.concatenate([mine, piece])
            bit = order[last - 1 - step]
        else:
            pieces = after(token, (kept[g], arriving[g]))
            update = update_columns(
                weights[order], pieces, update, start, width, update_scale
            )
            continue
        arriving[g] = flip(outgoing, devices, bit)
        token = outgoing
    return (
        update,
        jnp.concatenate(first_parts, axis=1),
        jnp.concatenate(second_parts, axis=1),
    )


def solution(mesh):
    dims = mesh_dims(mesh.shape["dp"])
    return jax.shard_map(
        functools.partial(local, dims),
        mesh=mesh,
        in_specs=(
            P("dp", "tensor"),
            P("dp", "tensor"),
            P("dp", None),
            P("dp", "tensor"),
            P("dp", "tensor"),
        ),
        out_specs=(P("dp", "tensor"), P("dp", "tensor"), P("dp", "tensor")),
        check_vma=False,
    )
```

```python
import functools
import itertools
import math

import jax
import jax.numpy as jnp
from jax import lax
from jax.experimental import pallas as pl
from jax.experimental.pallas import tpu as pltpu
from jax.sharding import PartitionSpec as P

BETA_ONE = 0.9
BETA_TWO = 0.999
CORRECT_ONE = 0.9999999993
CORRECT_TWO = 0.18135117
EPSILON = 1e-08

HIGHEST = lax.Precision.HIGHEST
F32 = jnp.float32
BF16 = jnp.bfloat16
BLOCK = 128
PIVOTS = 8
VMEM_LIMIT = 40 << 20

GROUPS = ((2, (2, 1, 0, 3)), (2, (1, 0, 2, 3)), (2, (0, 1, 2, 3)), (2, (2, 0, 1, 3)))
STEPS = ((0, 0), (1, 0), (2, 0), (3, 0), (0, 1), (1, 1), (2, 1), (0, 2), (1, 2), (3, 1), (0, 3), (2, 2), (1, 3), (0, 4), (2, 3), (3, 2), (1, 4), (3, 3), (0, 5), (2, 4), (0, 6), (1, 5), (3, 4), (2, 5), (0, 7), (1, 6), (3, 5), (2, 6), (3, 6), (1, 7), (2, 7), (3, 7), (0, 8), (1, 8), (2, 8), (3, 8))


GATHER = ((3, (0, 1, 2, 3)), (3, (1, 0, 2, 3)), (2, (2, 1, 0, 3)))


def flip_pairs(devices, bit):
    return [(at, at ^ (1 << bit)) for at in range(devices)]


def flip(value, devices, bit):
    return lax.ppermute(value, "dp", flip_pairs(devices, bit))


def mesh_dims(devices):
    if devices == 16:
        return (4, 2, 2)
    if devices == 64:
        return (4, 4, 4)
    return (devices, 1, 1)


def shift_pairs(dims, shift):
    pairs = []
    for place in itertools.product(*(range(size) for size in dims)):
        target = [(at + by) % size for at, by, size in zip(place, shift, dims)]
        pairs.append((flat(place, dims), flat(target, dims)))
    return pairs


def flat(place, dims):
    index = 0
    for at, size in zip(place, dims):
        index = index * size + at
    return index


def send(value, dims, shift):
    return lax.ppermute(value, "dp", shift_pairs(dims, shift))


def dot_nn(a, b):
    return lax.dot_general(
        a, b, (((1,), (0,)), ((), ())), precision=HIGHEST, preferred_element_type=F32
    )


def dot_nt(a, b):
    return lax.dot_general(
        a, b, (((1,), (1,)), ((), ())), precision=HIGHEST, preferred_element_type=F32
    )


def inverse_factor(block):
    size = block.shape[0]
    tiles = size // 8
    lane = lax.broadcasted_iota(jnp.int32, (8, size), 1)
    sub = lax.broadcasted_iota(jnp.int32, (8, size), 0)
    spread = lambda value: jnp.broadcast_to(value, (8, size))
    work = [block[8 * i : 8 * i + 8, :] for i in range(tiles)]
    scale = [jnp.zeros((8, size), F32) for _ in range(tiles)]
    for base in range(0, size, PIVOTS):
        first = base // 8
        cols = {
            (i, k): spread(work[i][:, base + k : base + k + 1])
            for i in range(first, tiles)
            for k in range(PIVOTS)
        }
        for k in range(PIVOTS):
            j = base + k
            r, q = j % 8, j // 8
            pivot = spread(cols[q, k][r : r + 1, :])
            recip = 1.0 / pivot
            row = jnp.where(lane == j, 1.0, spread(work[q][r : r + 1, :]))
            later = {m: spread(cols[q, m][r : r + 1, :]) for m in range(k + 1, PIVOTS)}
            scale[q] = jnp.where(sub == r, pivot, scale[q])
            for i in range(q, tiles):
                ratio = cols[i, k] * recip
                cleared = lane == j
                if i == q:
                    ratio = jnp.where(sub > r, ratio, 0.0)
                    cleared = cleared & (sub > r)
                for m in range(k + 1, PIVOTS):
                    cols[i, m] = cols[i, m] - ratio * later[m]
                work[i] = jnp.where(cleared, 0.0, work[i]) - ratio * row
    out = []
    for i in range(tiles):
        at = sub + 8 * i
        lower = jnp.where(lane == at, 1.0, jnp.where(lane < at, work[i], 0.0))
        out.append(lower * lax.rsqrt(scale[i]))
    return jnp.concatenate(out, axis=0)


def lower_blocks(size):
    return [(i, j) for i in range(size // BLOCK) for j in range(i + 1)]


def factor_steps(first, last, work_ref, out_ref):
    size = out_ref.shape[0]

    def step(at, carry):
        base = pl.multiple_of(at * BLOCK, BLOCK)
        inverse = inverse_factor(work_ref[pl.ds(base, BLOCK), pl.ds(base, BLOCK)])
        rows = dot_nn(inverse, out_ref[pl.ds(base, BLOCK), :])
        out_ref[pl.ds(base, BLOCK), :] = rows

        @pl.when(at < size // BLOCK - 1)
        def _():
            panel = dot_nt(work_ref[:, pl.ds(base, BLOCK)], inverse)
            below = lax.broadcasted_iota(jnp.int32, (size, BLOCK), 0) >= base + BLOCK
            panel = jnp.where(below, panel, 0.0)
            work_ref[...] -= dot_nt(panel, panel)
            out_ref[...] -= dot_nn(panel, rows)

        return carry

    lax.fori_loop(first, last, step, 0)


def factor_head(blocks, steps, packed_ref, work_ref, out_ref):
    size = out_ref.shape[0]
    work_ref[...] = jnp.zeros_like(work_ref)
    for at, (i, j) in enumerate(blocks):
        work_ref[i * BLOCK : (i + 1) * BLOCK, j * BLOCK : (j + 1) * BLOCK] = packed_ref[
            at * BLOCK : (at + 1) * BLOCK, :
        ]
    out_ref[...] = jnp.where(
        lax.broadcasted_iota(jnp.int32, (size, size), 0)
        == lax.broadcasted_iota(jnp.int32, (size, size), 1),
        1.0,
        0.0,
    )
    factor_steps(0, steps, work_ref, out_ref)


def factor_rest(steps, start_ref, done_ref, out_ref, work_ref):
    work_ref[...] = start_ref[...]
    out_ref[...] = done_ref[...]
    factor_steps(steps, out_ref.shape[0] // BLOCK, work_ref, out_ref)


def head_of_factor(packed, blocks, size, steps):
    square = jax.ShapeDtypeStruct((size, size), F32)
    return pl.pallas_call(
        functools.partial(factor_head, blocks, steps),
        out_shape=(square, square),
        in_specs=[pl.BlockSpec(memory_space=pltpu.VMEM)],
        out_specs=(pl.BlockSpec(memory_space=pltpu.VMEM),) * 2,
        compiler_params=pltpu.CompilerParams(vmem_limit_bytes=VMEM_LIMIT),
        name="factor_head",
    )(packed)


def rest_of_factor(work, done, steps):
    return pl.pallas_call(
        functools.partial(factor_rest, steps),
        out_shape=jax.ShapeDtypeStruct(work.shape, F32),
        in_specs=[pl.BlockSpec(memory_space=pltpu.VMEM)] * 2,
        out_specs=pl.BlockSpec(memory_space=pltpu.VMEM),
        scratch_shapes=[pltpu.VMEM(work.shape, F32)],
        compiler_params=pltpu.CompilerParams(vmem_limit_bytes=VMEM_LIMIT),
        name="factor_rest",
    )(work, done)


def gram_and_sketch(sketch, half, dims, own, core):
    devices = math.prod(dims)
    bits = devices.bit_length() - 1
    size = sketch.shape[1]
    blocks = lower_blocks(size)
    split = len(blocks) // 2
    gram = jnp.dot(sketch.T, sketch, precision=HIGHEST, preferred_element_type=F32)
    tiles = [
        gram[i * BLOCK : (i + 1) * BLOCK, j * BLOCK : (j + 1) * BLOCK] for i, j in blocks
    ]
    mine = jnp.where(
        core == 0, jnp.concatenate(tiles[:split]), jnp.concatenate(tiles[split:])
    )
    plane = dims[1] * dims[2]
    share = mine.shape[0] // plane
    at_of = lambda a, b: ((own[1] + a) % dims[1] * dims[2] + (own[2] + b) % dims[2]) * share
    shifts = list(itertools.product(range(dims[1]), range(dims[2])))
    part = lambda a, b: lax.dynamic_slice_in_dim(mine, at_of(a, b), share, 0)
    outgoing = [part(a, b) for a, b in shifts[1:]]
    total = part(0, 0)
    arrived = [send(piece, dims, (0, a, b)) for (a, b), piece in zip(shifts[1:], outgoing)]

    groups = gather_groups(half.shape[0], bits)
    (half,) = after(outgoing[-1], (half,))
    parts = [(groups, half[None], flip(half[None], devices, groups[0][1][-1]))]

    def widen(stage, token, chosen=slice(None)):
        split = []
        for members, rows, piece in parts[chosen]:
            rows, piece = after(token, (rows, piece))
            token = jnp.concatenate([rows, piece])
            start = 0
            for bit, same in itertools.groupby(members, lambda m: m[1][-1 - stage]):
                same = list(same)
                tall = sum(rows for rows, _ in same)
                piece = token[:, start : start + tall]
                start += tall
                split.append((same, piece, flip(piece, devices, bit)))
        parts[chosen] = split
        return token

    arrived = after(half, arrived)
    for piece in arrived:
        total = total + piece
    arrived = [send(total, dims, (by, 0, 0)) for by in range(1, dims[0])]
    token = widen(1, arrived[0])
    arrived = after(token, arrived)
    places = jnp.stack([total, *arrived])
    order = [(own[0] - z) % dims[0] for z in range(dims[0])]
    total = functools.reduce(
        jnp.add, [lax.dynamic_index_in_dim(places, at, 0, keepdims=False) for at in order]
    )
    arrived = [send(total, dims, (0, -a, -b)) for a, b in shifts[1:]]
    token = widen(2, arrived[0], slice(0, max(1, len(parts) - 1)))
    arrived = after(token, arrived)
    whole = lax.dynamic_update_slice_in_dim(
        jnp.zeros_like(mine), total, at_of(0, 0), 0
    )
    for (a, b), piece in zip(shifts[1:], arrived):
        whole = lax.dynamic_update_slice_in_dim(whole, piece, at_of(a, b), 0)
    other = lax.ppermute(whole, "tensor", [(0, 1), (1, 0)])
    token = whole
    if len(parts) > 2:
        token = widen(2, token, slice(-1, None))
    for stage in range(3, bits - 1):
        token = widen(stage, token)
    whole, other = after(token, (whole, other))
    packed = jnp.where(
        core == 0, jnp.concatenate([whole, other]), jnp.concatenate([other, whole])
    )
    work, done = head_of_factor(packed, blocks, size, 2)
    token = widen(bits - 1, work)
    work, done = after(token, (work, done))
    inverse = rest_of_factor(work, done, 2)
    orders = [order for _, order in groups]
    return inverse, orders, [part[1] for part in parts], [part[2] for part in parts]


def gather_groups(rows, bits):
    chosen = GATHER if rows >= 4 * BLOCK else ((8, GATHER[0][1]),)
    return [(share * rows // 8, order + tuple(range(4, bits))) for share, order in chosen]


def mix_kernel(groups, limit, table_ref, left_ref, right_ref, *refs):
    at = pl.program_id(0)
    out_ref = refs[-1]
    total = None
    for side, source in enumerate((left_ref, right_ref)):
        rows = []
        for g in range(groups):
            near, far = refs[2 * g], refs[2 * g + 1]
            place = table_ref[side, g, at]
            far_place = lax.rem(place, limit)
            rows.append(jnp.where(place < limit, near[far_place], far[far_place]))
        term = jnp.dot(
            source[...], jnp.concatenate(rows, axis=0), preferred_element_type=F32
        )
        total = term if total is None else total + term

    @pl.when(at == 0)
    def _():
        out_ref[...] = total

    @pl.when(at > 0)
    def _():
        out_ref[...] += total


def mix(left, right, near, far, groups, dp, core):
    limit, _, cols = near[0].shape
    bits = limit.bit_length()
    count = len(groups)
    blocks = jnp.arange(limit, dtype=jnp.int32)
    table = []
    for side in (core, 1 - core):
        apart = (side * limit + blocks) ^ dp
        row = []
        for order in groups:
            place = jnp.zeros_like(apart)
            for bit in order:
                place = place * 2 + ((apart >> bit) & 1)
            row.append(place)
        table.append(jnp.stack(row))
    table = jnp.stack(table)
    block = left.shape[1] // limit
    in_specs = [pl.BlockSpec((left.shape[0], block), lambda i, t: (0, i))] * 2
    operands = [left, right]
    for g in range(count):
        spec = pl.BlockSpec(near[g].shape, lambda i, t: (0, 0, 0))
        in_specs += [spec, spec]
        operands += [near[g], far[g]]
    return pl.pallas_call(
        functools.partial(mix_kernel, count, limit),
        grid_spec=pltpu.PrefetchScalarGridSpec(
            num_scalar_prefetch=1,
            grid=(limit,),
            in_specs=in_specs,
            out_specs=pl.BlockSpec((left.shape[0], cols), lambda i, t: (0, 0)),
        ),
        out_shape=jax.ShapeDtypeStruct((left.shape[0], cols), F32),
        compiler_params=pltpu.CompilerParams(vmem_limit_bytes=VMEM_LIMIT),
        name="mix",
    )(table, *operands)


def update_kernel(scale, count, *refs):
    weight_ref, pieces, out_ref = refs[0], refs[1 : 1 + count], refs[-1]
    rows = pieces[0].shape[0]
    total = None
    for at, piece in enumerate(pieces):
        term = jnp.dot(
            weight_ref[:, at * rows : (at + 1) * rows],
            piece[...],
            preferred_element_type=F32,
        )
        total = term if total is None else total + term
    out_ref[...] = scale * total


def update_columns(weight, pieces, previous, start, width, scale):
    tall, rank = weight.shape
    rows, cols = pieces[0].shape
    wide = min(1024, cols)
    first = start // wide
    in_specs = [pl.BlockSpec((tall, rank), lambda j: (0, 0))]
    in_specs += [pl.BlockSpec((rows, wide), lambda j: (0, j)) for _ in pieces]
    operands = [weight, *pieces]
    aliases = {}
    if previous is not None:
        aliases = {len(operands): 0}
        in_specs.append(pl.BlockSpec(memory_space=pl.ANY))
        operands.append(previous)
    return pl.pallas_call(
        functools.partial(update_kernel, scale, len(pieces)),
        grid=(cols // wide,),
        out_shape=jax.ShapeDtypeStruct((tall, width), F32),
        in_specs=in_specs,
        out_specs=pl.BlockSpec((tall, wide), lambda j: (0, first + j)),
        input_output_aliases=aliases,
        compiler_params=pltpu.CompilerParams(vmem_limit_bytes=VMEM_LIMIT),
        name="update_columns",
    )(*operands)


def selection(devices, dp, order, rank):
    index = jnp.zeros((), jnp.int32)
    for bit in order:
        index = index[..., None] | jnp.array([0, 1 << bit], jnp.int32)
    piece = rank // devices
    index = (index ^ dp)[..., None] * piece + jnp.arange(piece, dtype=jnp.int32)
    index = index.reshape(rank)
    return (index[:, None] == jnp.arange(rank, dtype=jnp.int32)[None, :]).astype(BF16)


def after(token, values):
    if token is None:
        return values
    return lax.optimization_barrier((*values, token))[:-1]


def local(dims, activations, out_grads, sketch, first_moment, second_moment):
    devices = math.prod(dims)
    bits = devices.bit_length() - 1
    dp = lax.axis_index("dp")
    core = lax.axis_index("tensor")
    own = (dp // (dims[1] * dims[2]), dp // dims[2] % dims[1], dp % dims[2])
    rank = sketch.shape[1]
    width = out_grads.shape[1]
    depth = activations.shape[1] * 2

    beside = lax.ppermute(activations, "tensor", [(0, 1), (1, 0)])
    half = lax.dynamic_slice_in_dim(sketch, core * (rank // 2), rank // 2, 1).astype(BF16)
    inverse, groups, near, far = gram_and_sketch(sketch, half, dims, own, core)
    *far, activations = after(inverse, (*far, activations))
    mixed_half = mix(activations, beside, near, far, groups, dp, core)
    mixed_other = lax.ppermute(mixed_half, "tensor", [(0, 1), (1, 0)])
    mixed = jnp.where(
        core == 0,
        jnp.concatenate([mixed_half, mixed_other], axis=1),
        jnp.concatenate([mixed_other, mixed_half], axis=1),
    )

    orders = [order + tuple(range(4, bits)) for _, order in GROUPS]
    picks = {order: selection(devices, dp, order, rank) for order in orders}
    projected, weights = {}, {}
    update_scale = math.sqrt(depth / rank)
    eighth = width // 8
    starts = [sum(share for share, _ in GROUPS[:g]) * eighth for g in range(len(GROUPS))]
    kept = [None] * len(GROUPS)
    arriving = [None] * len(GROUPS)
    first_parts = [None] * len(GROUPS)
    second_parts = [None] * len(GROUPS)
    token = None
    update = None
    last = 2 * bits
    steps = STEPS if STEPS and bits == 4 else [
        (g, s) for s in range(last + 1) for g in range(len(GROUPS))
    ]
    for g, step in steps:
        order = orders[g]
        if step == 1 and not weights:
            rows, factor = after(token, (sketch, inverse))
            own_rows = dot_nt(rows, factor).astype(BF16)
            for each, pick in picks.items():
                weights[each] = lax.dot_general(
                    own_rows, pick, (((1,), (1,)), ((), ())), preferred_element_type=F32
                ).astype(BF16)
            token = tuple(weights.values())
        cols = GROUPS[g][0] * eighth
        start = starts[g]
        columns = slice(start, start + cols)
        if step == 0:
            size = rank // 2
            (grads,) = after(token, (out_grads,))
            if not projected:
                turned = lax.dot_general(
                    picks[order].astype(F32),
                    inverse,
                    (((1,), (0,)), ((), ())),
                    precision=lax.Precision.HIGH,
                    preferred_element_type=F32,
                )
                projected[order] = lax.dot_general(
                    turned,
                    mixed,
                    (((1,), (1,)), ((), ())),
                    precision=lax.Precision.HIGH,
                    preferred_element_type=F32,
                ).astype(BF16)
            elif order not in projected:
                base, rows = next(iter(projected.items()))
                (rows,) = after(token, (rows,))
                bare = rows.reshape((2,) * bits + (rank // devices, rows.shape[1]))
                axes = [base.index(bit) for bit in order] + [bits, bits + 1]
                projected[order] = bare.transpose(axes).reshape(rows.shape)
            left = projected[order]
            outgoing = jnp.dot(
                left[size:], grads[:, columns], preferred_element_type=F32
            ).astype(BF16)
            grads, left, outgoing = lax.optimization_barrier((grads, left, outgoing))
            kept[g] = jnp.dot(left[:size], grads[:, columns], preferred_element_type=F32)
            bit = order[0]
        elif step < bits:
            total, piece = after(token, (kept[g], arriving[g]))
            total = total + piece.astype(F32)
            size = total.shape[0] // 2
            outgoing = total[size:].astype(BF16)
            kept[g] = total[:size]
            bit = order[step]
        elif step == bits:
            total, piece = after(token, (kept[g], arriving[g]))
            grad_low = total + piece.astype(F32)
            first = BETA_ONE * first_moment[:, columns] + (1.0 - BETA_ONE) * grad_low
            second = (
                BETA_TWO * second_moment[:, columns]
                + (1.0 - BETA_TWO) * grad_low * grad_low
            )
            outgoing = (
                first / CORRECT_ONE / (jnp.sqrt(second / CORRECT_TWO) + EPSILON)
            ).astype(BF16)
            first_parts[g], second_parts[g] = first, second
            kept[g] = outgoing
            bit = order[bits - 1]
        elif step < last:
            mine, piece = after(token, (kept[g], arriving[g]))
            outgoing = kept[g] = jnp.concatenate([mine, piece])
            bit = order[last - 1 - step]
        else:
            pieces = after(token, (kept[g], arriving[g]))
            update = update_columns(
                weights[order], pieces, update, start, width, update_scale
            )
            continue
        arriving[g] = flip(outgoing, devices, bit)
        token = outgoing
    return (
        update,
        jnp.concatenate(first_parts, axis=1),
        jnp.concatenate(second_parts, axis=1),
    )


def solution(mesh):
    dims = mesh_dims(mesh.shape["dp"])
    return jax.shard_map(
        functools.partial(local, dims),
        mesh=mesh,
        in_specs=(
            P("dp", "tensor"),
            P("dp", "tensor"),
            P("dp", None),
            P("dp", "tensor"),
            P("dp", "tensor"),
        ),
        out_specs=(P("dp", "tensor"), P("dp", "tensor"), P("dp", "tensor")),
        check_vma=False,
    )
```
